512 devices in a mesh: depth: 64 (over z, y), strip: 8 (over x, core).
Axes of the slice: x: 4, y: 8, z: 8, core: 2. Of those that a mesh axis runs over, the one named last changes fastest.
Arguments:
- volume: float32 [128, 512, 1024], P('strip', 'depth'), may hold values from -4.5 to 6.5
- extinction: float32 [1], replicated, may hold values from 0.0005859375 to 0.001953125
- color_map: float32 [3, 2], replicated, may hold values from -3 to 3
- light_direction: float32 [3], replicated, may hold values from -4 to 4
Outputs:
- image: float32 [4, 128, 1024], P(None, 'strip', 'depth')
The draws below stay inside these ranges and needn't reach their ends.
All inputs are finite; a program needn't handle non-finite values.
Results may differ from the reference program's by a relative error of at most 0.000034.
Values sent between devices are 32-bit elements; how exact they have to be, the bound alone decides.
No kernel may reach another device: no remote copies, remote signals or barrier semaphores. Data moves between devices by JAX's collectives and lax.ppermute only.
A program may use at most 64 MiB of HBM per device.

```python
import math
import jax
import jax.numpy as jnp
from jax import lax

ROWS_DEV = 16
DEPTH_DEV = 8
W = 1024
NR = 128
NZ = 512


def draw_volume(key, part):
    offset_key = jax.random.fold_in(key, 11)
    rough_key = jax.random.fold_in(key, 23)
    levels = jax.random.uniform(offset_key, (NR // ROWS_DEV, NZ // DEPTH_DEV), jnp.float32, -0.5, 2.5)
    levels = jnp.repeat(jnp.repeat(levels, ROWS_DEV, axis=0), DEPTH_DEV, axis=1)
    rough_part = jnp.clip(jax.random.normal(rough_key, (NR, NZ, W), jnp.float32), -4.0, 4.0)
    return (levels[:, :, None] + rough_part).astype(jnp.float32)


def draw_light_direction(key, part):
    sign_key = jax.random.fold_in(key, 37)
    size_key = jax.random.fold_in(key, 41)
    signs = jnp.where(jax.random.uniform(sign_key, (3,), jnp.float32) < 0.5, -1.0, 1.0)
    magnitude = jnp.exp(jax.random.uniform(size_key, (3,), jnp.float32, 0.0, 1.3862944))
    return (signs * magnitude).astype(jnp.float32)


def setup_inputs(seed: int = 0) -> dict:
    key_of = jax.random.split(jax.random.key(seed), 5)
    return {
        "volume": draw_volume(jax.random.fold_in(key_of[4], 71), 0),
        "extinction": jnp.clip(jnp.exp(jax.random.uniform(key_of[1], (1,), jnp.float32, math.log(0.0005859375), math.log(0.001953125))), 0.0005859375, 0.001953125),
        "color_map": jnp.clip(jax.random.uniform(key_of[2], (3, 2), jnp.float32, -3.0, 3.0), -3.0, 3.0),
        "light_direction": draw_light_direction(jax.random.fold_in(key_of[4], 71), 0),
    }


def blur_valid(field_in, along):
    extent = field_in.shape[along]
    lower_cells = lax.slice_in_dim(field_in, 0, extent - 2, axis=along)
    middle = lax.slice_in_dim(field_in, 1, extent - 1, axis=along)
    upper_cells = lax.slice_in_dim(field_in, 2, extent, axis=along)
    return 0.25 * lower_cells + 0.5 * middle + 0.25 * upper_cells


def slope_valid(field_in, along):
    extent = field_in.shape[along]
    lower_cells = lax.slice_in_dim(field_in, 0, extent - 2, axis=along)
    upper_cells = lax.slice_in_dim(field_in, 2, extent, axis=along)
    return 0.5 * (upper_cells - lower_cells)


def smooth_all(padded):
    return blur_valid(blur_valid(blur_valid(padded, 0), 1), 2)


def gradients(padded):
    first = blur_valid(blur_valid(slope_valid(padded, 0), 1), 2)
    second = blur_valid(blur_valid(slope_valid(padded, 1), 0), 2)
    third = blur_valid(blur_valid(slope_valid(padded, 2), 0), 1)
    return first, second, third


def render_slab(smoothed, gradient, extinction, color_map, light_direction):
    facing = gradient[0] * light_direction[0] + gradient[1] * light_direction[1] + gradient[2] * light_direction[2]
    shading = 0.3 + 0.7 * facing * facing / (1.0 + facing * facing)
    optical = extinction[0] * jax.nn.softplus(2.0 * smoothed)
    opacity = 1.0 - jnp.exp(-optical)
    prior_depth = jnp.cumsum(optical, axis=1) - optical
    weights = jnp.exp(-prior_depth) * opacity * shading
    colors = jnp.stack([jnp.sum(weights * jax.nn.sigmoid(color_map[channel, 0] * smoothed + color_map[channel, 1]), axis=1) for channel in range(3)], 0)
    transmit = jnp.exp(-jnp.sum(optical, axis=1))
    return jnp.concatenate([colors, transmit[None]], 0)


def reference(volume, extinction, color_map, light_direction):
    smoothed = smooth_all(jnp.pad(volume, 1))
    gradient = gradients(jnp.pad(smoothed, 1))
    layer = render_slab(smoothed, gradient, extinction, color_map, light_direction)
    return jnp.concatenate([layer[:3], 1.0 - layer[3:]], 0)
```

```python
import functools

import jax
import jax.numpy as jnp
from jax import lax
from jax.experimental import pallas as pl
from jax.experimental.pallas import tpu as pltpu
from jax.sharding import PartitionSpec as P

ROWS, SLABS, SUB, LANE = 16, 8, 8, 128
VM = pl.BlockSpec(memory_space=pltpu.VMEM)
SM = pl.BlockSpec(memory_space=pltpu.SMEM)


def cells(x_ref, row, slab):
    return x_ref[pl.ds(row * 64 + slab, SUB, stride=SLABS), :]


def pack_depth(x_ref, low_ref, high_ref):
    for row in range(ROWS):
        for k in range(2):
            low_ref[k, row] = cells(x_ref, row, k)
            high_ref[k, row] = cells(x_ref, row, SLABS - 2 + k)


def pack_strip(x_ref, before_ref, after_ref, low_ref, high_ref):
    for k in range(2):
        low_ref[k] = before_ref[k, 0:2]
        high_ref[k] = before_ref[k, ROWS - 2 : ROWS]
        low_ref[SLABS + 2 + k] = after_ref[k, 0:2]
        high_ref[SLABS + 2 + k] = after_ref[k, ROWS - 2 : ROWS]
        for slab in range(SLABS):
            low_ref[2 + slab, k] = cells(x_ref, k, slab)
            high_ref[2 + slab, k] = cells(x_ref, ROWS - 2 + k, slab)


def column_neighbours(v):
    lane = lax.broadcasted_iota(jnp.int32, (SUB, LANE), 1)
    sub = lax.broadcasted_iota(jnp.int32, (SUB, LANE), 0)
    a = pltpu.roll(v, 1, 1)
    b = pltpu.roll(a, 1, 0)
    prev = jnp.where(lane == 0, jnp.where(sub == 0, 0.0, b), a)
    a = pltpu.roll(v, LANE - 1, 1)
    b = pltpu.roll(a, SUB - 1, 0)
    following = jnp.where(lane == LANE - 1, jnp.where(sub == SUB - 1, 0.0, b), a)
    return prev, following


def log1p_unit(e):
    t = e / (2.0 + e)
    q = t * t
    s = 1.0 / 13.0
    for d in (11.0, 9.0, 7.0, 5.0, 3.0):
        s = s * q + 1.0 / d
    return 2.0 * t + 2.0 * t * (q * s)


def render(ext_ref, cmap_ref, light_ref, edge_ref, x_ref, before_ref, after_ref,
           up_ref, down_ref, out_ref, z_ref, s_ref, ap_ref, am_ref, y_ref, part_ref):
    def slab_sums(v):
        e = [v[k] + v[k + 1] for k in range(SLABS + 3)]
        return [e[k] + e[k + 1] for k in range(SLABS + 2)]

    for k, ref in ((0, up_ref), (18, down_ref)):
        for j in range(2):
            z = slab_sums([ref[slab, j] for slab in range(SLABS + 4)])
            for slab in range(SLABS + 2):
                z_ref[k + j, slab] = z[slab]

    def first(row, _):
        v = [before_ref[k, row] for k in range(2)]
        v += [cells(x_ref, row, slab) for slab in range(SLABS)]
        v += [after_ref[k, row] for k in range(2)]
        z = slab_sums(v)
        for slab in range(SLABS + 2):
            z_ref[row + 2, slab] = z[slab]
        return 0

    lax.fori_loop(0, ROWS, first, 0)

    edge_up, edge_down, edge_before, edge_after = (edge_ref[i] for i in range(4))
    half_l0 = light_ref[0] * 0.5
    quarter_l1 = light_ref[1] * 0.5 * 0.25 * 0.25
    quarter_l2 = light_ref[2] * 0.5 * 0.25 * 0.25
    scale_p = half_l0 * 0.25 * 0.25

    def second(row, _):
        inside = jnp.where(row == 0, edge_up, jnp.where(row == ROWS + 1, edge_down, 1.0))
        scale = inside * (1.0 / 64.0)
        u, w = [], []
        for slab in range(SLABS + 2):
            mid = z_ref[row + 1, slab]
            m = (z_ref[row, slab] + mid) + (mid + z_ref[row + 2, slab])
            prev, following = column_neighbours(m)
            factor = scale
            if slab == 0:
                factor = scale * edge_before
            if slab == SLABS + 1:
                factor = scale * edge_after
            s = ((prev + following) + (m + m)) * factor
            if 1 <= slab <= SLABS:
                s_ref[row, slab - 1] = s
            prev, following = column_neighbours(s)
            u.append((prev + following) + (s + s))
            w.append(following - prev)
        for slab in range(SLABS):
            p = (u[slab] + u[slab + 1]) + (u[slab + 1] + u[slab + 2])
            q = u[slab + 2] - u[slab]
            t = (w[slab] + w[slab + 1]) + (w[slab + 1] + w[slab + 2])
            y = quarter_l1 * q + quarter_l2 * t
            p = scale_p * p
            ap_ref[row, slab] = y + p
            am_ref[row, slab] = y - p
            y_ref[row, slab] = y + y
        return 0

    lax.fori_loop(0, ROWS + 2, second, 0)

    ext = ext_ref[0]
    slopes = [cmap_ref[c, 0] * 0.5 for c in range(3)]
    offsets = [cmap_ref[c, 1] * 0.5 for c in range(3)]

    def third(row, _):
        through = None
        colors = [None] * 3
        for slab in range(SLABS):
            s = s_ref[row + 1, slab]
            facing = (ap_ref[row + 2, slab] + am_ref[row, slab]) + y_ref[row + 1, slab]
            shading = 1.0 - 0.7 / (1.0 + facing * facing)
            z = s + s
            soft = jnp.maximum(z, 0.0) + log1p_unit(jnp.exp(-jnp.abs(z)))
            clear = jnp.exp(-ext * soft)
            weight = (1.0 - clear) * shading
            if through is None:
                through = clear
            else:
                weight = weight * through
                through = through * clear
            for c in range(3):
                value = weight * (0.5 * jnp.tanh(slopes[c] * s + offsets[c]) + 0.5)
                colors[c] = value if colors[c] is None else colors[c] + value
        for c in range(3):
            part_ref[c, row] = colors[c]
        part_ref[3, row] = through
        return 0

    lax.fori_loop(0, ROWS, third, 0)

    chunk = lax.broadcasted_iota(jnp.int32, (SUB, LANE), 1) // 16
    for g in range(8):
        v = [part_ref[g // 2, (g % 2) * 8 + i] for i in range(8)]
        for bit in (4, 2, 1):
            upper = (chunk & bit) != 0
            for i in range(8):
                if i & bit == 0:
                    lo, hi = v[i], v[i + bit]
                    v[i] = jnp.where(upper, pltpu.roll(hi, 16 * bit, 1), lo)
                    v[i + bit] = jnp.where(upper, hi, pltpu.roll(lo, LANE - 16 * bit, 1))
        for m in range(8):
            out_ref[pl.ds(m * 8 + g, SUB, stride=64), :] = v[m]


def composite(parts_ref, out_ref, tmp_ref):
    sub = lax.broadcasted_iota(jnp.int32, (SUB, LANE), 0)
    is_clear = sub >= 6
    through = jnp.ones((SUB, LANE), jnp.float32)
    total = jnp.zeros((SUB, LANE), jnp.float32)
    for d in range(parts_ref.shape[0] // SUB):
        x = parts_ref[d * SUB : (d + 1) * SUB, :]
        total = total + through * x
        m = jnp.where(is_clear, x, 1.0)
        m = m * pltpu.roll(m, 2, 0)
        m = m * pltpu.roll(m, 4, 0)
        through = through * m
    result = jnp.where(is_clear, 1.0 - through, total)
    for i in range(8):
        moved = result if i == 0 else pltpu.roll(result, LANE - 16 * i, 1)
        tmp_ref[pl.ds(i, SUB, stride=SUB), :] = moved
    out_ref[...] = tmp_ref[:, 0:16]


def f32(*shape):
    return jax.ShapeDtypeStruct(shape, jnp.float32)


def local(volume, extinction, color_map, light_direction):
    strips, groups = lax.axis_size("strip"), lax.axis_size("depth")
    x = volume.reshape(ROWS, SLABS, SUB, LANE).transpose(0, 2, 1, 3).reshape(ROWS * 64, LANE)

    def pairs(count):
        forward = [(i, i + 1) for i in range(count - 1)]
        return forward, [(b, a) for a, b in forward]

    low, high = pl.pallas_call(
        pack_depth, in_specs=[VM], out_specs=[VM, VM], name="pack_depth",
        out_shape=[f32(2, ROWS, SUB, LANE)] * 2,
    )(x)
    forward, backward = pairs(groups)
    before = lax.ppermute(high, "depth", forward)
    after = lax.ppermute(low, "depth", backward)
    low, high = pl.pallas_call(
        pack_strip, in_specs=[VM] * 3, out_specs=[VM, VM], name="pack_strip",
        out_shape=[f32(SLABS + 4, 2, SUB, LANE)] * 2,
    )(x, before, after)
    forward, backward = pairs(strips)
    up = lax.ppermute(high, "strip", forward)
    down = lax.ppermute(low, "strip", backward)

    strip, group = lax.axis_index("strip"), lax.axis_index("depth")
    edges = jnp.stack([strip > 0, strip < strips - 1, group > 0, group < groups - 1])
    blocks = pl.pallas_call(
        render, in_specs=[SM] * 4 + [VM] * 5, out_specs=VM, name="render",
        out_shape=f32(groups * SUB, LANE),
        scratch_shapes=[
            pltpu.VMEM((ROWS + 4, SLABS + 2, SUB, LANE), jnp.float32),
            *[pltpu.VMEM((ROWS + 2, SLABS, SUB, LANE), jnp.float32)] * 4,
            pltpu.VMEM((4, ROWS, SUB, LANE), jnp.float32),
        ],
    )(extinction, color_map, light_direction, edges.astype(jnp.float32), x, before, after, up, down)
    layers = lax.all_to_all(
        blocks.reshape(groups, SUB, LANE), "depth", split_axis=0, concat_axis=0, tiled=True
    )
    image = pl.pallas_call(
        composite, in_specs=[VM], out_specs=VM, name="composite",
        out_shape=f32(64, 16), scratch_shapes=[pltpu.VMEM((64, LANE), jnp.float32)],
    )(layers.reshape(groups * SUB, LANE))
    return image.reshape(4, 16, 16)


def solution(mesh):
    in_specs = (P("strip", "depth", None), P(), P(), P())
    out_specs = P(None, "strip", "depth")
    return jax.shard_map(local, mesh=mesh, in_specs=in_specs, out_specs=out_specs, check_vma=False)
```

```python
import jax
import jax.numpy as jnp
from jax import lax
from jax.experimental import pallas as pl
from jax.experimental.pallas import tpu as pltpu
from jax.sharding import PartitionSpec as P

ROWS, SLABS, SUB, LANE = 16, 8, 8, 128
VM = pl.BlockSpec(memory_space=pltpu.VMEM)
SM = pl.BlockSpec(memory_space=pltpu.SMEM)


def cells(x_ref, row, slab):
    return x_ref[pl.ds(row * 64 + slab, SUB, stride=SLABS), :]


def parity(axis):
    return lax.axis_index(axis) % 2


def pack_depth(x_ref, first_ref, second_ref):
    odd = parity("depth")
    start = (SLABS - 2) * (1 - odd)
    for row in range(ROWS):
        for k in range(2):
            first_ref[k, row] = cells(x_ref, row, start + k)
            second_ref[k, row] = cells(x_ref, row, (SLABS - 2) - start + k)


def by_parity(odd, first, second):
    is_odd = odd == 1
    return jnp.where(is_odd, first, second), jnp.where(is_odd, second, first)


def pack_strip(x_ref, from_first_ref, from_second_ref, first_ref, second_ref):
    odd = parity("strip")
    group_odd = parity("depth")
    start = (ROWS - 2) * (1 - odd)
    for ref, row in ((first_ref, start), (second_ref, (ROWS - 2) - start)):
        for k in range(2):
            for j in range(2):
                before, after = by_parity(
                    group_odd, from_first_ref[j, row + k], from_second_ref[j, row + k]
                )
                ref[j, k] = before
                ref[SLABS + 2 + j, k] = after
            for slab in range(SLABS):
                ref[2 + slab, k] = cells(x_ref, row + k, slab)


def column_neighbours(v):
    lane = lax.broadcasted_iota(jnp.int32, (SUB, LANE), 1)
    sub = lax.broadcasted_iota(jnp.int32, (SUB, LANE), 0)
    a = pltpu.roll(v, 1, 1)
    b = pltpu.roll(a, 1, 0)
    prev = jnp.where(lane == 0, jnp.where(sub == 0, 0.0, b), a)
    a = pltpu.roll(v, LANE - 1, 1)
    b = pltpu.roll(a, SUB - 1, 0)
    following = jnp.where(lane == LANE - 1, jnp.where(sub == SUB - 1, 0.0, b), a)
    return prev, following


def log1p_unit(e):
    t = e / (2.0 + e)
    q = t * t
    s = 1.0 / 13.0
    for d in (11.0, 9.0, 7.0, 5.0, 3.0):
        s = s * q + 1.0 / d
    return 2.0 * t + 2.0 * t * (q * s)


def render(ext_ref, cmap_ref, light_ref, x_ref, depth_first_ref, depth_second_ref,
           strip_first_ref, strip_second_ref, out_ref, z_ref, s_ref, ap_ref, am_ref, y_ref,
           part_ref):
    odd_strip, odd_group = parity("strip"), parity("depth")

    def slab_sums(v):
        e = [v[k] + v[k + 1] for k in range(SLABS + 3)]
        return [e[k] + e[k + 1] for k in range(SLABS + 2)]

    def halo(row, ref):
        for j in range(2):
            z = slab_sums([ref[slab, j] for slab in range(SLABS + 4)])
            for slab in range(SLABS + 2):
                z_ref[row + j, slab] = z[slab]

    halo((ROWS + 2) * (1 - odd_strip), strip_first_ref)
    halo((ROWS + 2) * odd_strip, strip_second_ref)

    def first(row, _):
        ends = [by_parity(odd_group, depth_first_ref[k, row], depth_second_ref[k, row]) for k in range(2)]
        v = [before for before, _ in ends]
        v += [cells(x_ref, row, slab) for slab in range(SLABS)]
        v += [after for _, after in ends]
        z = slab_sums(v)
        for slab in range(SLABS + 2):
            z_ref[row + 2, slab] = z[slab]
        return 0

    lax.fori_loop(0, ROWS, first, 0)

    strip, strips = lax.axis_index("strip"), lax.axis_size("strip")
    group, groups = lax.axis_index("depth"), lax.axis_size("depth")
    edge_up = jnp.where(strip == 0, 0.0, 1.0)
    edge_down = jnp.where(strip == strips - 1, 0.0, 1.0)
    edge_before = jnp.where(group == 0, 0.0, 1.0)
    edge_after = jnp.where(group == groups - 1, 0.0, 1.0)
    half_l0 = light_ref[0] * 0.5
    quarter_l1 = light_ref[1] * 0.5 * 0.25 * 0.25
    quarter_l2 = light_ref[2] * 0.5 * 0.25 * 0.25
    scale_p = half_l0 * 0.25 * 0.25

    def second(row, _):
        inside = jnp.where(row == 0, edge_up, jnp.where(row == ROWS + 1, edge_down, 1.0))
        scale = inside * (1.0 / 64.0)
        u, w = [], []
        for slab in range(SLABS + 2):
            mid = z_ref[row + 1, slab]
            m = (z_ref[row, slab] + mid) + (mid + z_ref[row + 2, slab])
            prev, following = column_neighbours(m)
            factor = scale
            if slab == 0:
                factor = scale * edge_before
            if slab == SLABS + 1:
                factor = scale * edge_after
            s = ((prev + following) + (m + m)) * factor
            if 1 <= slab <= SLABS:
                s_ref[row, slab - 1] = s
            prev, following = column_neighbours(s)
            u.append((prev + following) + (s + s))
            w.append(following - prev)
        for slab in range(SLABS):
            p = (u[slab] + u[slab + 1]) + (u[slab + 1] + u[slab + 2])
            q = u[slab + 2] - u[slab]
            t = (w[slab] + w[slab + 1]) + (w[slab + 1] + w[slab + 2])
            y = quarter_l1 * q + quarter_l2 * t
            p = scale_p * p
            ap_ref[row, slab] = y + p
            am_ref[row, slab] = y - p
            y_ref[row, slab] = y + y
        return 0

    lax.fori_loop(0, ROWS + 2, second, 0)

    ext = ext_ref[0]
    slopes = [cmap_ref[c, 0] * 0.5 for c in range(3)]
    offsets = [cmap_ref[c, 1] * 0.5 for c in range(3)]

    def third(row, _):
        through = None
        colors = [None] * 3
        for slab in range(SLABS):
            s = s_ref[row + 1, slab]
            facing = (ap_ref[row + 2, slab] + am_ref[row, slab]) + y_ref[row + 1, slab]
            shading = 1.0 - 0.7 / (1.0 + facing * facing)
            z = s + s
            soft = jnp.maximum(z, 0.0) + log1p_unit(jnp.exp(-jnp.abs(z)))
            clear = jnp.exp(-ext * soft)
            weight = (1.0 - clear) * shading
            if through is None:
                through = clear
            else:
                weight = weight * through
                through = through * clear
            for c in range(3):
                value = weight * (0.5 * jnp.tanh(slopes[c] * s + offsets[c]) + 0.5)
                colors[c] = value if colors[c] is None else colors[c] + value
        for c in range(3):
            part_ref[c, row] = colors[c]
        part_ref[3, row] = through
        return 0

    lax.fori_loop(0, ROWS, third, 0)

    chunk = lax.broadcasted_iota(jnp.int32, (SUB, LANE), 1) // 16
    for g in range(8):
        v = [part_ref[g // 2, (g % 2) * 8 + i] for i in range(8)]
        for bit in (4, 2, 1):
            upper = (chunk & bit) != 0
            for i in range(8):
                if i & bit == 0:
                    lo, hi = v[i], v[i + bit]
                    v[i] = jnp.where(upper, pltpu.roll(hi, 16 * bit, 1), lo)
                    v[i + bit] = jnp.where(upper, hi, pltpu.roll(lo, LANE - 16 * bit, 1))
        for m in range(8):
            out_ref[pl.ds(m * 8 + g, SUB, stride=64), :] = v[m]


def composite(parts_ref, out_ref, tmp_ref):
    sub = lax.broadcasted_iota(jnp.int32, (SUB, LANE), 0)
    is_clear = sub >= 6
    through = jnp.ones((SUB, LANE), jnp.float32)
    total = jnp.zeros((SUB, LANE), jnp.float32)
    for d in range(parts_ref.shape[0] // SUB):
        x = parts_ref[d * SUB : (d + 1) * SUB, :]
        total = total + through * x
        m = jnp.where(is_clear, x, 1.0)
        m = m * pltpu.roll(m, 2, 0)
        m = m * pltpu.roll(m, 4, 0)
        through = through * m
    result = jnp.where(is_clear, 1.0 - through, total)
    for i in range(8):
        moved = result if i == 0 else pltpu.roll(result, LANE - 16 * i, 1)
        tmp_ref[pl.ds(i, SUB, stride=SUB), :] = moved
    out_ref[...] = tmp_ref[:, 0:16]


def f32(*shape):
    return pltpu.VMEM(shape, jnp.float32)


def near(*arrays):
    return [pltpu.with_memory_space_constraint(a, pltpu.VMEM) for a in arrays]


def local(volume, extinction, color_map, light_direction):
    groups = lax.axis_size("depth")
    (x,) = near(volume.reshape(ROWS, SLABS, SUB, LANE).transpose(0, 2, 1, 3).reshape(ROWS * 64, LANE))

    def swaps(count):
        out = []
        for start in range(2):
            half = [(i, i + 1) for i in range(start, count - 1, 2)]
            out.append(half + [(b, a) for a, b in half])
        return out

    def exchange(buffers, axis):
        return near(*[lax.ppermute(v, axis, p) for v, p in zip(buffers, swaps(lax.axis_size(axis)))])

    near_depth = exchange(
        pl.pallas_call(
            pack_depth, in_specs=[VM], out_specs=[VM, VM], name="pack_depth",
            out_shape=[f32(2, ROWS, SUB, LANE)] * 2,
        )(x),
        "depth",
    )
    near_strip = exchange(
        pl.pallas_call(
            pack_strip, in_specs=[VM] * 3, out_specs=[VM, VM], name="pack_strip",
            out_shape=[f32(SLABS + 4, 2, SUB, LANE)] * 2,
        )(x, *near_depth),
        "strip",
    )
    blocks = pl.pallas_call(
        render, in_specs=[SM] * 3 + [VM] * 5, out_specs=VM, name="render",
        out_shape=f32(groups * SUB, LANE),
        scratch_shapes=[
            pltpu.VMEM((ROWS + 4, SLABS + 2, SUB, LANE), jnp.float32),
            *[pltpu.VMEM((ROWS + 2, SLABS, SUB, LANE), jnp.float32)] * 4,
            pltpu.VMEM((4, ROWS, SUB, LANE), jnp.float32),
        ],
    )(extinction, color_map, light_direction, x, *near_depth, *near_strip)
    layers = lax.all_to_all(
        blocks.reshape(groups, SUB, LANE), "depth", split_axis=0, concat_axis=0, tiled=True
    )
    image = pl.pallas_call(
        composite, in_specs=[VM], out_specs=VM, name="composite",
        out_shape=jax.ShapeDtypeStruct((64, 16), jnp.float32), scratch_shapes=[pltpu.VMEM((64, LANE), jnp.float32)],
    )(*near(layers.reshape(groups * SUB, LANE)))
    return image.reshape(4, 16, 16)


def solution(mesh):
    in_specs = (P("strip", "depth", None), P(), P(), P())
    out_specs = P(None, "strip", "depth")
    return jax.shard_map(local, mesh=mesh, in_specs=in_specs, out_specs=out_specs, check_vma=False)
```

```python
import jax
import jax.numpy as jnp
from jax import lax
from jax.experimental import pallas as pl
from jax.experimental.pallas import tpu as pltpu
from jax.sharding import PartitionSpec as P

ROWS, SLABS, SUB, LANE = 16, 8, 8, 128
VM = pl.BlockSpec(memory_space=pltpu.VMEM)
SM = pl.BlockSpec(memory_space=pltpu.SMEM)


SMALL = pltpu.CompilerParams(vmem_limit_bytes=4 << 20)


def cells(x_ref, row, slab):
    return x_ref[pl.ds(row * 64 + slab, SUB, stride=SLABS), :]


def parity(axis):
    return lax.axis_index(axis) % 2


def pack_depth(x_ref, first_ref, second_ref):
    odd = parity("depth")
    start = (SLABS - 2) * (1 - odd)
    for row in range(ROWS):
        for k in range(2):
            first_ref[k, row] = cells(x_ref, row, start + k)
            second_ref[k, row] = cells(x_ref, row, (SLABS - 2) - start + k)


def by_parity(odd, first, second):
    is_odd = odd == 1
    return jnp.where(is_odd, first, second), jnp.where(is_odd, second, first)


def pack_strip(x_ref, from_first_ref, from_second_ref, _, first_ref, second_ref):
    odd = parity("strip")
    group_odd = parity("depth")
    start = (ROWS - 2) * (1 - odd)
    for ref, row in ((first_ref, start), (second_ref, (ROWS - 2) - start)):
        for k in range(2):
            for j in range(2):
                before, after = by_parity(
                    group_odd, from_first_ref[j, row + k], from_second_ref[j, row + k]
                )
                ref[j, k] = before
                ref[SLABS + 2 + j, k] = after
            for slab in range(SLABS):
                ref[2 + slab, k] = cells(x_ref, row + k, slab)


def column_neighbours(v):
    lane = lax.broadcasted_iota(jnp.int32, (SUB, LANE), 1)
    sub = lax.broadcasted_iota(jnp.int32, (SUB, LANE), 0)
    a = pltpu.roll(v, 1, 1)
    b = pltpu.roll(a, 1, 0)
    prev = jnp.where(lane == 0, jnp.where(sub == 0, 0.0, b), a)
    a = pltpu.roll(v, LANE - 1, 1)
    b = pltpu.roll(a, SUB - 1, 0)
    following = jnp.where(lane == LANE - 1, jnp.where(sub == SUB - 1, 0.0, b), a)
    return prev, following


def log1p_unit(e):
    t = e / (2.0 + e)
    q = t * t
    s = 1.0 / 13.0
    for d in (11.0, 9.0, 7.0, 5.0, 3.0):
        s = s * q + 1.0 / d
    return 2.0 * t + 2.0 * t * (q * s)


def smoothed(lower, middle, upper, factor):
    m = (lower + middle) + (middle + upper)
    prev, following = column_neighbours(m)
    return ((prev + following) + (m + m)) * factor


def column_parts(s):
    prev, following = column_neighbours(s)
    return (prev + following) + (s + s), following - prev


def gradient_parts(u, w, light):
    p = (u[0] + u[1]) + (u[1] + u[2])
    q = u[2] - u[0]
    t = (w[0] + w[1]) + (w[1] + w[2])
    scale = 0.5 * 0.25 * 0.25
    y = (light[1] * scale) * q + (light[2] * scale) * t
    p = (light[0] * scale) * p
    return y + p, y - p, y + y


def shade(s, facing, ext, slopes, offsets):
    shading = 1.0 - 0.7 / (1.0 + facing * facing)
    z = s + s
    soft = jnp.maximum(z, 0.0) + log1p_unit(jnp.exp(-jnp.abs(z)))
    clear = jnp.exp(-ext * soft)
    weight = (1.0 - clear) * shading
    return [weight * (0.5 * jnp.tanh(a * s + b) + 0.5) for a, b in zip(slopes, offsets)] + [clear]


def over(front, back):
    if front is None:
        return back
    through = front[3]
    return [f + through * c for f, c in zip(front[:3], back[:3])] + [through * back[3]]


def coefficients(ext_ref, cmap_ref, light_ref):
    light = [light_ref[i] for i in range(3)]
    slopes = [cmap_ref[c, 0] * 0.5 for c in range(3)]
    offsets = [cmap_ref[c, 1] * 0.5 for c in range(3)]
    return light, (ext_ref[0], slopes, offsets)


def ends_inside(axis):
    index, count = lax.axis_index(axis), lax.axis_size(axis)
    return jnp.where(index == 0, 0.0, 1.0), jnp.where(index == count - 1, 0.0, 1.0)


def binomial(v):
    e = [a + b for a, b in zip(v, v[1:])]
    return [a + b for a, b in zip(e, e[1:])]


def render_inner(ext_ref, cmap_ref, light_ref, x_ref, _, z_ref, u_ref, w_ref, ap_ref, am_ref, y_ref,
                 s_ref, mid_ref):
    light, color = coefficients(ext_ref, cmap_ref, light_ref)

    def first(row, _):
        z = binomial([cells(x_ref, row, slab) for slab in range(SLABS)])
        for i, v in enumerate(z):
            z_ref[row, i] = v
        return 0

    lax.fori_loop(0, ROWS, first, 0)

    def second(row, _):
        s = [
            smoothed(z_ref[row - 1, i], z_ref[row, i], z_ref[row + 1, i], 1.0 / 64.0)
            for i in range(6)
        ]
        u, w = zip(*[column_parts(v) for v in s])
        for i, k in enumerate((0, 1, 4, 5)):
            u_ref[row, i] = u[k]
            w_ref[row, i] = w[k]
        for i in range(4):
            ap, am, y = gradient_parts(u[i : i + 3], w[i : i + 3], light)
            ap_ref[row, i] = ap
            am_ref[row, i] = am
            y_ref[row, i] = y
        for i in range(6):
            s_ref[row, i] = s[i]
        return 0

    lax.fori_loop(1, ROWS - 1, second, 0)

    def third(row, _):
        total = None
        for i in range(4):
            facing = (ap_ref[row + 1, i] + am_ref[row - 1, i]) + y_ref[row, i]
            total = over(total, shade(s_ref[row, i + 1], facing, *color))
        for c in range(4):
            mid_ref[c, row] = total[c]
        return 0

    lax.fori_loop(2, ROWS - 2, third, 0)


def render_outer(ext_ref, cmap_ref, light_ref, x_ref, depth_first_ref, depth_second_ref, ui_ref,
                 wi_ref, si_ref, mid_ref, z_ref, ap_ref, am_ref, y_ref, s_ref, part_ref):
    light, color = coefficients(ext_ref, cmap_ref, light_ref)
    odd_group = parity("depth")
    edge_before, edge_after = ends_inside("depth")

    def first(row, _):
        ends = [
            by_parity(odd_group, depth_first_ref[k, row], depth_second_ref[k, row])
            for k in range(2)
        ]
        z = binomial([ends[0][0], ends[1][0], cells(x_ref, row, 0), cells(x_ref, row, 1)])
        z += binomial([cells(x_ref, row, 6), cells(x_ref, row, 7), ends[0][1], ends[1][1]])
        for i, v in enumerate(z):
            z_ref[row, i] = v
        return 0

    lax.fori_loop(0, ROWS, first, 0)

    def second(row, _):
        edges = (edge_before, None, None, edge_after)
        s = []
        for i, edge in enumerate(edges):
            factor = 1.0 / 64.0 if edge is None else edge * (1.0 / 64.0)
            s.append(smoothed(z_ref[row - 1, i], z_ref[row, i], z_ref[row + 1, i], factor))
        u, w = zip(*[column_parts(v) for v in s])
        ui = [ui_ref[row, i] for i in range(4)]
        wi = [wi_ref[row, i] for i in range(4)]
        u = [u[0], u[1], ui[0], ui[1]], [ui[2], ui[3], u[2], u[3]]
        w = [w[0], w[1], wi[0], wi[1]], [wi[2], wi[3], w[2], w[3]]
        for side in range(2):
            for j in range(2):
                i = 2 * side + j
                ap, am, y = gradient_parts(u[side][j : j + 3], w[side][j : j + 3], light)
                ap_ref[row, i] = ap
                am_ref[row, i] = am
                y_ref[row, i] = y
        s_ref[row, 0] = s[1]
        s_ref[row, 1] = s[2]
        return 0

    lax.fori_loop(1, ROWS - 1, second, 0)

    def third(row, _):
        smooth = [s_ref[row, 0], si_ref[row, 0], si_ref[row, 5], s_ref[row, 1]]
        total = None
        for i in range(4):
            if i == 2:
                total = over(total, [mid_ref[c, row] for c in range(4)])
            facing = (ap_ref[row + 1, i] + am_ref[row - 1, i]) + y_ref[row, i]
            total = over(total, shade(smooth[i], facing, *color))
        for c in range(4):
            part_ref[c, row] = total[c]
        return 0

    lax.fori_loop(2, ROWS - 2, third, 0)


def render_rows(ext_ref, cmap_ref, light_ref, strip_first_ref, strip_second_ref, zi_ref, api_ref,
                ami_ref, yi_ref, si_ref, zo_ref, apo_ref, amo_ref, yo_ref, so_ref, part_ref,
                out_ref, halo_ref, here_ref, s_ref, all_ref):
    light, color = coefficients(ext_ref, cmap_ref, light_ref)
    odd_strip = parity("strip")
    edge_before, edge_after = ends_inside("depth")
    edge_up, edge_down = ends_inside("strip")

    for base, ref in ((2 * (1 - odd_strip), strip_first_ref), (2 * odd_strip, strip_second_ref)):
        for j in range(2):
            for i, v in enumerate(binomial([ref[slab, j] for slab in range(SLABS + 4)])):
                halo_ref[base + j, i] = v

    def sums(row, slab):
        if row < 0:
            return halo_ref[row + 2, slab + 1]
        if row >= ROWS:
            return halo_ref[row - ROWS + 2, slab + 1]
        if 1 <= slab <= 6:
            return zi_ref[row, slab - 1]
        return zo_ref[row, slab + 1 if slab < 1 else slab - 5]

    def kept(inner_ref, outer_ref, row, slab):
        if 2 <= slab <= 5:
            return inner_ref[row, slab - 2]
        return outer_ref[row, slab if slab < 2 else slab - 4]

    def kept_smooth(row, slab):
        return si_ref[row, slab - 1] if 1 <= slab <= 6 else so_ref[row, slab // 7]

    for n, row in enumerate((-1, 0, ROWS - 1, ROWS)):
        outside = {-1: edge_up, ROWS: edge_down}.get(row)
        u, w = [], []
        for slab in range(-1, SLABS + 1):
            factor = 1.0 / 64.0
            for edge in (outside, {-1: edge_before, SLABS: edge_after}.get(slab)):
                factor = factor if edge is None else factor * edge
            v = smoothed(sums(row - 1, slab), sums(row, slab), sums(row + 1, slab), factor)
            if 0 <= slab < SLABS and 0 <= row < ROWS:
                s_ref[n - 1, slab] = v
            a, b = column_parts(v)
            u.append(a)
            w.append(b)
        for slab in range(SLABS):
            for i, v in enumerate(gradient_parts(u[slab : slab + 3], w[slab : slab + 3], light)):
                here_ref[n, i, slab] = v

    for row in (0, 1, ROWS - 2, ROWS - 1):
        total = None
        for slab in range(SLABS):
            if row == 0:
                facing = kept(api_ref, apo_ref, 1, slab) + here_ref[0, 1, slab] + here_ref[1, 2, slab]
            elif row == 1:
                facing = kept(api_ref, apo_ref, 2, slab) + here_ref[1, 1, slab] + kept(yi_ref, yo_ref, 1, slab)
            elif row == ROWS - 2:
                facing = here_ref[2, 0, slab] + kept(ami_ref, amo_ref, row - 1, slab) + kept(yi_ref, yo_ref, row, slab)
            else:
                facing = here_ref[3, 0, slab] + kept(ami_ref, amo_ref, row - 1, slab) + here_ref[2, 2, slab]
            s = s_ref[row // 8, slab] if row in (0, ROWS - 1) else kept_smooth(row, slab)
            total = over(total, shade(s, facing, *color))
        for c in range(4):
            all_ref[(c * ROWS + row) * SUB : (c * ROWS + row + 1) * SUB, :] = total[c]
    for c in range(4):
        for row in range(2, ROWS - 2):
            all_ref[(c * ROWS + row) * SUB : (c * ROWS + row + 1) * SUB, :] = part_ref[c, row]

    chunk = lax.broadcasted_iota(jnp.int32, (SUB, LANE), 1) // 16
    for tile in range(SUB):
        v = [all_ref[pl.ds(g * 64 + tile, SUB, stride=SUB), :] for g in range(8)]
        for bit in (4, 2, 1):
            upper = (chunk & bit) != 0
            for i in range(8):
                if i & bit == 0:
                    lo, hi = v[i], v[i + bit]
                    v[i] = jnp.where(upper, pltpu.roll(hi, 16 * bit, 1), lo)
                    v[i + bit] = jnp.where(upper, hi, pltpu.roll(lo, LANE - 16 * bit, 1))
        for m in range(8):
            row = (tile * 8 + m) * SUB
            out_ref[row : row + SUB, :] = v[m]


def composite(parts_ref, out_ref):
    is_clear = lax.broadcasted_iota(jnp.int32, (SUB, LANE), 1) >= 96
    through = jnp.ones((SUB, LANE), jnp.float32)
    total = jnp.zeros((SUB, LANE), jnp.float32)
    for d in range(parts_ref.shape[0] // SUB):
        x = parts_ref[d * SUB : (d + 1) * SUB, :]
        total = total + through * x
        m = jnp.where(is_clear, x, 1.0)
        m = m * pltpu.roll(m, 32, 1)
        m = m * pltpu.roll(m, 64, 1)
        through = through * m
    result = jnp.where(is_clear, 1.0 - through, total)
    for i in range(8):
        moved = result if i == 0 else pltpu.roll(result, LANE - 16 * i, 1)
        out_ref[i * SUB : (i + 1) * SUB, :] = moved[:, 0:16]


def f32(*shape):
    return pltpu.VMEM(shape, jnp.float32)


def near(*arrays):
    return [pltpu.with_memory_space_constraint(a, pltpu.VMEM) for a in arrays]


def local(volume, extinction, color_map, light_direction):
    groups = lax.axis_size("depth")
    x = volume.reshape(ROWS, SLABS, SUB, LANE).transpose(0, 2, 1, 3).reshape(ROWS * 64, LANE)

    def swaps(count):
        out = []
        for start in range(2):
            half = [(i, i + 1) for i in range(start, count - 1, 2)]
            out.append(half + [(b, a) for a, b in half])
        return out

    def exchange(buffers, axis):
        return [lax.ppermute(v, axis, p) for v, p in zip(buffers, swaps(lax.axis_size(axis)))]

    packed = pl.pallas_call(
        pack_depth, in_specs=[VM], compiler_params=SMALL, out_specs=[VM, VM], name="pack_depth",
        out_shape=[f32(2, ROWS, SUB, LANE)] * 2,
    )(*near(x))
    near_depth = exchange(packed, "depth")

    params = (extinction, color_map, light_direction)

    def kernel(body, operands, shapes, scratch=()):
        return pl.pallas_call(
            body, in_specs=[SM] * 3 + [VM] * len(operands), out_specs=[VM] * len(shapes),
            name=body.__name__, compiler_params=SMALL, out_shape=[f32(*shape) for shape in shapes],
            scratch_shapes=[f32(*shape) for shape in scratch],
        )(*params, *near(*operands))

    four = (ROWS, 4, SUB, LANE)
    zi, ui, wi, api, ami, yi, si, mid = kernel(
        render_inner, (x, packed[0]),
        [(ROWS, 6, SUB, LANE)] + [four] * 5 + [(ROWS, 6, SUB, LANE), (4, ROWS, SUB, LANE)],
    )
    near_strip = exchange(
        pl.pallas_call(
            pack_strip, in_specs=[VM] * 4, compiler_params=SMALL, out_specs=[VM, VM], name="pack_strip",
            out_shape=[f32(SLABS + 4, 2, SUB, LANE)] * 2,
        )(*near(x, *near_depth, mid)),
        "strip",
    )
    zo, apo, amo, yo, so, part = kernel(
        render_outer, (x, *near_depth, ui, wi, si, mid),
        [four] * 4 + [(ROWS, 2, SUB, LANE), (4, ROWS, SUB, LANE)],
    )
    (blocks,) = kernel(
        render_rows, (*near_strip, zi, api, ami, yi, si, zo, apo, amo, yo, so, part),
        [(groups * SUB, LANE)],
        [(4, SLABS + 2, SUB, LANE), (4, 3, SLABS, SUB, LANE), (2, SLABS, SUB, LANE),
         (4 * ROWS * SUB, LANE)],
    )
    layers = lax.all_to_all(
        blocks.reshape(groups, SUB, LANE), "depth", split_axis=0, concat_axis=0, tiled=True
    )
    image = pl.pallas_call(
        composite, in_specs=[VM], compiler_params=SMALL, out_specs=VM, name="composite",
        out_shape=jax.ShapeDtypeStruct((64, 16), jnp.float32),
    )(*near(layers.reshape(groups * SUB, LANE)))
    return image.reshape(4, 16, 16)


def solution(mesh):
    in_specs = (P("strip", "depth", None), P(), P(), P())
    out_specs = P(None, "strip", "depth")
    return jax.shard_map(local, mesh=mesh, in_specs=in_specs, out_specs=out_specs, check_vma=False)
```

```python
import jax
import jax.numpy as jnp
from jax import lax
from jax.experimental import pallas as pl
from jax.experimental.pallas import tpu as pltpu
from jax.sharding import PartitionSpec as P

ROWS, SLABS, SUB, LANE = 16, 8, 8, 128
PAIR = 2
VM = pl.BlockSpec(memory_space=pltpu.VMEM)
SM = pl.BlockSpec(memory_space=pltpu.SMEM)


SMALL = pltpu.CompilerParams(vmem_limit_bytes=4 << 20)


def cells(x_ref, row, slab):
    return x_ref[pl.ds(row * 64 + slab, SUB, stride=SLABS), :]


def parity(axis):
    return lax.axis_index(axis) % 2


def pack_depth(x_ref, first_ref, second_ref):
    odd = parity("depth")
    start = (SLABS - 2) * (1 - odd)
    for row in range(ROWS):
        for k in range(2):
            first_ref[k, row] = cells(x_ref, row, start + k)
            second_ref[k, row] = cells(x_ref, row, (SLABS - 2) - start + k)


def by_parity(odd, first, second):
    is_odd = odd == 1
    return jnp.where(is_odd, first, second), jnp.where(is_odd, second, first)


def pack_strip(x_ref, from_first_ref, from_second_ref, _, first_ref, second_ref):
    odd = parity("strip")
    group_odd = parity("depth")
    start = (ROWS - 2) * (1 - odd)
    for ref, row in ((first_ref, start), (second_ref, (ROWS - 2) - start)):
        for k in range(2):
            for j in range(2):
                before, after = by_parity(
                    group_odd, from_first_ref[j, row + k], from_second_ref[j, row + k]
                )
                ref[j, k] = before
                ref[SLABS + 2 + j, k] = after
            for slab in range(SLABS):
                ref[2 + slab, k] = cells(x_ref, row + k, slab)


def rolled(v, shift, axis):
    return pltpu.roll(v.reshape(-1, SUB, LANE), shift, axis + 1).reshape(v.shape)


def column_neighbours(v):
    lane = lax.broadcasted_iota(jnp.int32, v.shape, v.ndim - 1)
    sub = lax.broadcasted_iota(jnp.int32, v.shape, v.ndim - 2)
    a = rolled(v, 1, 1)
    prev = jnp.where(lane == 0, jnp.where(sub == 0, 0.0, rolled(a, 1, 0)), a)
    a = rolled(v, LANE - 1, 1)
    following = jnp.where(lane == LANE - 1, jnp.where(sub == SUB - 1, 0.0, rolled(a, SUB - 1, 0)), a)
    return prev, following


def log1p_unit(e):
    t = e / (2.0 + e)
    q = t * t
    s = 1.0 / 13.0
    for d in (11.0, 9.0, 7.0, 5.0, 3.0):
        s = s * q + 1.0 / d
    return 2.0 * t + 2.0 * t * (q * s)


def row_sums(z):
    e = z[:-1] + z[1:]
    return e[:-1] + e[1:]


def slab_sums(v):
    e = v[:, :-1] + v[:, 1:]
    return e[:, :-1] + e[:, 1:]


def smoothed(m, factor):
    prev, following = column_neighbours(m)
    return ((prev + following) + (m + m)) * factor


def column_parts(s):
    prev, following = column_neighbours(s)
    return (prev + following) + (s + s), following - prev


def gradient_parts(u, w, light):
    scale = 0.5 * 0.25 * 0.25
    y = (light[1] * scale) * (u[:, 2:] - u[:, :-2]) + (light[2] * scale) * slab_sums(w)
    p = (light[0] * scale) * slab_sums(u)
    return y + p, y - p, y + y


def shade(s, facing, front, ext, slopes, offsets):
    half = 0.5 - 0.35 / (1.0 + facing * facing)
    z = s + s
    soft = jnp.maximum(z, 0.0) + log1p_unit(jnp.exp(-jnp.abs(z)))
    clear = jnp.exp(-ext * soft)
    weight = (1.0 - clear) * half
    tones = [jnp.tanh(a * s + b) + 1.0 for a, b in zip(slopes, offsets)]
    total = front
    for k in range(s.shape[1]):
        if total is None:
            total = [weight[:, k] * t[:, k] for t in tones] + [clear[:, k]]
        else:
            here = weight[:, k] * total[3]
            total = [c + here * t[:, k] for c, t in zip(total, tones)] + [total[3] * clear[:, k]]
    return total


def over(front, back):
    through = front[3]
    return [f + through * c for f, c in zip(front[:3], back[:3])] + [through * back[3]]


def coefficients(ext_ref, cmap_ref, light_ref):
    light = [light_ref[i] for i in range(3)]
    slopes = [cmap_ref[c, 0] * 0.5 for c in range(3)]
    offsets = [cmap_ref[c, 1] * 0.5 for c in range(3)]
    return light, (ext_ref[0], slopes, offsets)


def ends_inside(axis):
    index, count = lax.axis_index(axis), lax.axis_size(axis)
    return jnp.where(index == 0, 0.0, 1.0), jnp.where(index == count - 1, 0.0, 1.0)


def binomial(v):
    e = [a + b for a, b in zip(v, v[1:])]
    return [a + b for a, b in zip(e, e[1:])]


def render_inner(ext_ref, cmap_ref, light_ref, x_ref, _, z_ref, u_ref, w_ref, ap_ref, am_ref, y_ref,
                 s_ref, mid_ref):
    light, color = coefficients(ext_ref, cmap_ref, light_ref)

    def first(i, _):
        for row in (2 * i, 2 * i + 1):
            z = binomial([cells(x_ref, row, slab) for slab in range(SLABS)])
            for i, v in enumerate(z):
                z_ref[row, i] = v
        return 0

    lax.fori_loop(0, ROWS // 2, first, 0)

    def second(i, _):
        row = PAIR * i + 1
        s = smoothed(row_sums(z_ref[pl.ds(row - 1, PAIR + 2)]), 1.0 / 64.0)
        u, w = column_parts(s)
        here = pl.ds(row, PAIR)
        for i, k in enumerate((0, 1, 4, 5)):
            u_ref[here, i] = u[:, k]
            w_ref[here, i] = w[:, k]
        ap_ref[here], am_ref[here], y_ref[here] = gradient_parts(u, w, light)
        s_ref[here] = s
        return 0

    lax.fori_loop(0, (ROWS - 2) // PAIR, second, 0)

    def third(i, _):
        row = 2 * i + 2
        here = pl.ds(row, 2)
        facing = (ap_ref[pl.ds(row + 1, 2)] + am_ref[pl.ds(row - 1, 2)]) + y_ref[here]
        total = shade(s_ref[here, 1:5], facing, None, *color)
        for c in range(4):
            mid_ref[c, here] = total[c]
        return 0

    lax.fori_loop(0, (ROWS - 4) // 2, third, 0)


def render_outer(ext_ref, cmap_ref, light_ref, x_ref, depth_first_ref, depth_second_ref, zi_ref,
                 ui_ref, wi_ref, api_ref, ami_ref, yi_ref, si_ref, mid_ref, part_ref, zk_ref,
                 facing_ref, sk_ref, z_ref, ap_ref, am_ref, y_ref, s_ref):
    light, color = coefficients(ext_ref, cmap_ref, light_ref)
    odd_group = parity("depth")
    edge_before, edge_after = ends_inside("depth")

    def first(i, _):
        for row in (2 * i, 2 * i + 1):
            ends = [
                by_parity(odd_group, depth_first_ref[k, row], depth_second_ref[k, row])
                for k in range(2)
            ]
            z = binomial([ends[0][0], ends[1][0], cells(x_ref, row, 0), cells(x_ref, row, 1)])
            z += binomial([cells(x_ref, row, 6), cells(x_ref, row, 7), ends[0][1], ends[1][1]])
            z_ref[row, 0] = z[0] * edge_before
            z_ref[row, 1] = z[1]
            z_ref[row, 2] = z[2]
            z_ref[row, 3] = z[3] * edge_after
        return 0

    lax.fori_loop(0, ROWS // 2, first, 0)

    def second(i, _):
        row = PAIR * i + 1
        here = pl.ds(row, PAIR)
        s = smoothed(row_sums(z_ref[pl.ds(row - 1, PAIR + 2)]), 1.0 / 64.0)
        u, w = column_parts(s)
        for side in range(2):
            at = pl.ds(2 * side, 2)
            if side == 0:
                us = jnp.concatenate([u[:, 0:2], ui_ref[here, 0:2]], 1)
                ws = jnp.concatenate([w[:, 0:2], wi_ref[here, 0:2]], 1)
            else:
                us = jnp.concatenate([ui_ref[here, 2:4], u[:, 2:4]], 1)
                ws = jnp.concatenate([wi_ref[here, 2:4], w[:, 2:4]], 1)
            ap_ref[here, at], am_ref[here, at], y_ref[here, at] = gradient_parts(us, ws, light)
        s_ref[here, 0] = s[:, 1]
        s_ref[here, 1] = si_ref[here, 0]
        s_ref[here, 2] = si_ref[here, 5]
        s_ref[here, 3] = s[:, 2]
        return 0

    lax.fori_loop(0, (ROWS - 2) // PAIR, second, 0)

    def third(i, _):
        row = 2 * i + 2
        here = pl.ds(row, 2)
        facing = (ap_ref[pl.ds(row + 1, 2)] + am_ref[pl.ds(row - 1, 2)]) + y_ref[here]
        s = s_ref[here]
        front = shade(s[:, 0:2], facing[:, 0:2], None, *color)
        total = over(front, [mid_ref[c, here] for c in range(4)])
        total = shade(s[:, 2:4], facing[:, 2:4], total, *color)
        for c in range(4):
            part_ref[c, here] = total[c]
        return 0

    lax.fori_loop(0, (ROWS - 4) // 2, third, 0)

    def whole(inner, outer):
        return jnp.concatenate([outer[0:2], inner, outer[2:4]], 0)

    for i, row in enumerate((0, 1, ROWS - 2, ROWS - 1)):
        zk_ref[i] = whole(zi_ref[row], z_ref[row])
    facing_ref[0] = whole(api_ref[1], ap_ref[1])
    facing_ref[1] = whole(api_ref[2] + yi_ref[1], ap_ref[2] + y_ref[1])
    facing_ref[2] = whole(ami_ref[ROWS - 3] + yi_ref[ROWS - 2], am_ref[ROWS - 3] + y_ref[ROWS - 2])
    facing_ref[3] = whole(ami_ref[ROWS - 2], am_ref[ROWS - 2])
    for i, row in enumerate((1, ROWS - 2)):
        sk_ref[i, 0] = s_ref[row, 0]
        sk_ref[i, 1:7] = si_ref[row]
        sk_ref[i, 7] = s_ref[row, 3]


def render_rows(ext_ref, cmap_ref, light_ref, strip_first_ref, strip_second_ref, part_ref, zk_ref,
                facing_ref, sk_ref, out_ref, halo_ref, all_ref):
    light, color = coefficients(ext_ref, cmap_ref, light_ref)
    odd_strip = parity("strip")
    edge_before, edge_after = ends_inside("depth")
    edge_up, edge_down = ends_inside("strip")

    for base, ref in ((2 * (1 - odd_strip), strip_first_ref), (2 * odd_strip, strip_second_ref)):
        for j in range(2):
            z = binomial([ref[slab, j] for slab in range(SLABS + 4)])
            z[0] = z[0] * edge_before
            z[-1] = z[-1] * edge_after
            for i, v in enumerate(z):
                halo_ref[base + j, i] = v

    def row_parts(lower, middle, upper, factor):
        s = smoothed((lower + middle) + (middle + upper), factor)[None]
        u, w = column_parts(s)
        return s[:, 1:-1], *gradient_parts(u, w, light)

    def finish(row, s, facing):
        total = shade(s, facing, None, *color)
        for c in range(4):
            all_ref[(c * ROWS + row) * SUB : (c * ROWS + row + 1) * SUB, :] = total[c][0]

    _, _, above, _ = row_parts(halo_ref[0], halo_ref[1], zk_ref[0], edge_up * (1.0 / 64.0))
    s, _, am, y = row_parts(halo_ref[1], zk_ref[0], zk_ref[1], 1.0 / 64.0)
    finish(0, s, facing_ref[0:1] + above + y)
    finish(1, sk_ref[0:1], facing_ref[1:2] + am)
    _, below, _, _ = row_parts(zk_ref[3], halo_ref[2], halo_ref[3], edge_down * (1.0 / 64.0))
    s, ap, _, y = row_parts(zk_ref[2], zk_ref[3], halo_ref[2], 1.0 / 64.0)
    finish(ROWS - 1, s, facing_ref[3:4] + below + y)
    finish(ROWS - 2, sk_ref[1:2], facing_ref[2:3] + ap)
    for c in range(4):
        for row in range(2, ROWS - 2):
            all_ref[(c * ROWS + row) * SUB : (c * ROWS + row + 1) * SUB, :] = part_ref[c, row]

    chunk = lax.broadcasted_iota(jnp.int32, (SUB, LANE), 1) // 16
    for tile in range(SUB):
        v = [all_ref[pl.ds(g * 64 + tile, SUB, stride=SUB), :] for g in range(8)]
        for bit in (4, 2, 1):
            upper = (chunk & bit) != 0
            for i in range(8):
                if i & bit == 0:
                    lo, hi = v[i], v[i + bit]
                    v[i] = jnp.where(upper, pltpu.roll(hi, 16 * bit, 1), lo)
                    v[i + bit] = jnp.where(upper, hi, pltpu.roll(lo, LANE - 16 * bit, 1))
        for m in range(8):
            row = (tile * 8 + m) * SUB
            out_ref[row : row + SUB, :] = v[m]


def composite(parts_ref, out_ref):
    is_clear = lax.broadcasted_iota(jnp.int32, (SUB, LANE), 1) >= 96
    through = jnp.ones((SUB, LANE), jnp.float32)
    total = jnp.zeros((SUB, LANE), jnp.float32)
    for d in range(parts_ref.shape[0] // SUB):
        x = parts_ref[d * SUB : (d + 1) * SUB, :]
        total = total + through * x
        m = jnp.where(is_clear, x, 1.0)
        m = m * pltpu.roll(m, 32, 1)
        m = m * pltpu.roll(m, 64, 1)
        through = through * m
    result = jnp.where(is_clear, 1.0 - through, total)
    for i in range(8):
        moved = result if i == 0 else pltpu.roll(result, LANE - 16 * i, 1)
        out_ref[i * SUB : (i + 1) * SUB, :] = moved[:, 0:16]


def f32(*shape):
    return pltpu.VMEM(shape, jnp.float32)


def near(*arrays):
    return [pltpu.with_memory_space_constraint(a, pltpu.VMEM) for a in arrays]


def local(volume, extinction, color_map, light_direction):
    groups = lax.axis_size("depth")
    x = volume.reshape(ROWS, SLABS, SUB, LANE).transpose(0, 2, 1, 3).reshape(ROWS * 64, LANE)

    def swaps(count):
        out = []
        for start in range(2):
            half = [(i, i + 1) for i in range(start, count - 1, 2)]
            out.append(half + [(b, a) for a, b in half])
        return out

    def exchange(buffers, axis):
        return [lax.ppermute(v, axis, p) for v, p in zip(buffers, swaps(lax.axis_size(axis)))]

    packed = pl.pallas_call(
        pack_depth, in_specs=[VM], compiler_params=SMALL, out_specs=[VM, VM], name="pack_depth",
        out_shape=[f32(2, ROWS, SUB, LANE)] * 2,
    )(*near(x))
    near_depth = exchange(packed, "depth")

    params = (extinction, color_map, light_direction)

    def kernel(body, operands, shapes, scratch=()):
        return pl.pallas_call(
            body, in_specs=[SM] * 3 + [VM] * len(operands), out_specs=[VM] * len(shapes),
            name=body.__name__, compiler_params=SMALL, out_shape=[f32(*shape) for shape in shapes],
            scratch_shapes=[f32(*shape) for shape in scratch],
        )(*params, *near(*operands))

    four = (ROWS, 4, SUB, LANE)
    zi, ui, wi, api, ami, yi, si, mid = kernel(
        render_inner, (x, packed[0]),
        [(ROWS, 6, SUB, LANE)] + [four] * 5 + [(ROWS, 6, SUB, LANE), (4, ROWS, SUB, LANE)],
    )
    near_strip = exchange(
        pl.pallas_call(
            pack_strip, in_specs=[VM] * 4, compiler_params=SMALL, out_specs=[VM, VM], name="pack_strip",
            out_shape=[f32(SLABS + 4, 2, SUB, LANE)] * 2,
        )(*near(x, *near_depth, mid)),
        "strip",
    )
    kept = kernel(
        render_outer, (x, *near_depth, zi, ui, wi, api, ami, yi, si, mid),
        [(4, ROWS, SUB, LANE), (4, SLABS + 2, SUB, LANE), (4, SLABS, SUB, LANE), (2, SLABS, SUB, LANE)],
        [four] * 5,
    )
    (blocks,) = kernel(
        render_rows, (*near_strip, *kept),
        [(groups * SUB, LANE)], [(4, SLABS + 2, SUB, LANE), (4 * ROWS * SUB, LANE)],
    )
    layers = lax.all_to_all(
        blocks.reshape(groups, SUB, LANE), "depth", split_axis=0, concat_axis=0, tiled=True
    )
    image = pl.pallas_call(
        composite, in_specs=[VM], compiler_params=SMALL, out_specs=VM, name="composite",
        out_shape=jax.ShapeDtypeStruct((64, 16), jnp.float32),
    )(*near(layers.reshape(groups * SUB, LANE)))
    return image.reshape(4, 16, 16)


def solution(mesh):
    in_specs = (P("strip", "depth", None), P(), P(), P())
    out_specs = P(None, "strip", "depth")
    return jax.shard_map(local, mesh=mesh, in_specs=in_specs, out_specs=out_specs, check_vma=False)
```

```python
import jax
import jax.numpy as jnp
from jax import lax
from jax.experimental import pallas as pl
from jax.experimental.pallas import tpu as pltpu
from jax.sharding import PartitionSpec as P


ROWS, SLABS, SUB, LANE = 16, 8, 8, 128
PAIR = 2
VM = pl.BlockSpec(memory_space=pltpu.VMEM)
SM = pl.BlockSpec(memory_space=pltpu.SMEM)


SMALL = pltpu.CompilerParams(vmem_limit_bytes=4 << 20)


def cells(x_ref, row, slab):
    return x_ref[pl.ds(row * 64 + slab, SUB, stride=SLABS), :]


def parity(axis):
    return lax.axis_index(axis) % 2


def pack_depth(x_ref, first_ref, second_ref):
    odd = parity("depth")
    start = (SLABS - 2) * (1 - odd)
    for row in range(ROWS):
        for k in range(2):
            first_ref[k, row] = cells(x_ref, row, start + k)
            second_ref[k, row] = cells(x_ref, row, (SLABS - 2) - start + k)


def by_parity(odd, first, second):
    is_odd = odd == 1
    return jnp.where(is_odd, first, second), jnp.where(is_odd, second, first)


def pack_strip(x_ref, from_first_ref, from_second_ref, _, first_ref, second_ref):
    odd = parity("strip")
    group_odd = parity("depth")
    start = (ROWS - 2) * (1 - odd)
    for ref, row in ((first_ref, start), (second_ref, (ROWS - 2) - start)):
        for k in range(2):
            for j in range(2):
                before, after = by_parity(
                    group_odd, from_first_ref[j, row + k], from_second_ref[j, row + k]
                )
                ref[j, k] = before
                ref[SLABS + 2 + j, k] = after
            for slab in range(SLABS):
                ref[2 + slab, k] = cells(x_ref, row + k, slab)


def rolled(v, shift, axis):
    return pltpu.roll(v.reshape(-1, SUB, LANE), shift, axis + 1).reshape(v.shape)


def column_neighbours(v):
    lane = lax.broadcasted_iota(jnp.int32, v.shape, v.ndim - 1)
    sub = lax.broadcasted_iota(jnp.int32, v.shape, v.ndim - 2)
    a = rolled(v, 1, 1)
    prev = jnp.where(lane == 0, jnp.where(sub == 0, 0.0, rolled(a, 1, 0)), a)
    a = rolled(v, LANE - 1, 1)
    following = jnp.where(lane == LANE - 1, jnp.where(sub == SUB - 1, 0.0, rolled(a, SUB - 1, 0)), a)
    return prev, following


def log1p_unit(e):
    w = 1.0 + e
    return jnp.log(w) + (e - (w - 1.0))


def row_sums(z):
    e = z[:-1] + z[1:]
    return e[:-1] + e[1:]


def slab_sums(v):
    e = v[:, :-1] + v[:, 1:]
    return e[:, :-1] + e[:, 1:]


def smoothed(m, factor):
    prev, following = column_neighbours(m)
    return ((prev + following) + (m + m)) * factor


def column_parts(s):
    prev, following = column_neighbours(s)
    return (prev + following) + (s + s), following - prev


def gradient_parts(u, w, light):
    scale = 0.5 * 0.25 * 0.25
    y = (light[1] * scale) * (u[:, 2:] - u[:, :-2]) + (light[2] * scale) * slab_sums(w)
    p = (light[0] * scale) * slab_sums(u)
    return y + p, y - p, y + y


def shade(s, facing, front, ext, slopes, offsets):
    half = 0.5 - 0.35 / (1.0 + facing * facing)
    z = s + s
    soft = jnp.maximum(z, 0.0) + log1p_unit(jnp.exp(-jnp.abs(z)))
    clear = jnp.exp(-ext * soft)
    weight = (1.0 - clear) * half
    tones = [jnp.tanh(a * s + b) + 1.0 for a, b in zip(slopes, offsets)]
    total = front
    for k in range(s.shape[1]):
        if total is None:
            total = [weight[:, k] * t[:, k] for t in tones] + [clear[:, k]]
        else:
            here = weight[:, k] * total[3]
            total = [c + here * t[:, k] for c, t in zip(total, tones)] + [total[3] * clear[:, k]]
    return total


def over(front, back):
    through = front[3]
    return [f + through * c for f, c in zip(front[:3], back[:3])] + [through * back[3]]


def coefficients(ext_ref, cmap_ref, light_ref):
    light = [light_ref[i] for i in range(3)]
    slopes = [cmap_ref[c, 0] * 0.5 for c in range(3)]
    offsets = [cmap_ref[c, 1] * 0.5 for c in range(3)]
    return light, (ext_ref[0], slopes, offsets)


def ends_inside(axis):
    index, count = lax.axis_index(axis), lax.axis_size(axis)
    return jnp.where(index == 0, 0.0, 1.0), jnp.where(index == count - 1, 0.0, 1.0)


def binomial(v):
    e = [a + b for a, b in zip(v, v[1:])]
    return [a + b for a, b in zip(e, e[1:])]


def render_inner(ext_ref, cmap_ref, light_ref, x_ref, _, z_ref, u_ref, w_ref, ap_ref, am_ref, y_ref,
                 s_ref, mid_ref):
    light, color = coefficients(ext_ref, cmap_ref, light_ref)

    def first(i, _):
        for row in (2 * i, 2 * i + 1):
            z = binomial([cells(x_ref, row, slab) for slab in range(SLABS)])
            for i, v in enumerate(z):
                z_ref[row, i] = v
        return 0

    lax.fori_loop(0, ROWS // 2, first, 0, unroll=True)

    def second(i, _):
        row = PAIR * i + 1
        s = smoothed(row_sums(z_ref[pl.ds(row - 1, PAIR + 2)]), 1.0 / 64.0)
        u, w = column_parts(s)
        here = pl.ds(row, PAIR)
        for i, k in enumerate((0, 1, 4, 5)):
            u_ref[here, i] = u[:, k]
            w_ref[here, i] = w[:, k]
        ap_ref[here], am_ref[here], y_ref[here] = gradient_parts(u, w, light)
        s_ref[here] = s
        return 0

    lax.fori_loop(0, (ROWS - 2) // PAIR, second, 0, unroll=True)

    def third(i, _):
        row = 2 * i + 2
        here = pl.ds(row, 2)
        facing = (ap_ref[pl.ds(row + 1, 2)] + am_ref[pl.ds(row - 1, 2)]) + y_ref[here]
        total = shade(s_ref[here, 1:5], facing, None, *color)
        for c in range(4):
            mid_ref[c, here] = total[c]
        return 0

    lax.fori_loop(0, (ROWS - 4) // 2, third, 0, unroll=True)


def render_outer(ext_ref, cmap_ref, light_ref, x_ref, depth_first_ref, depth_second_ref, zi_ref,
                 ui_ref, wi_ref, api_ref, ami_ref, yi_ref, si_ref, mid_ref, part_ref, zk_ref,
                 facing_ref, sk_ref, z_ref, ap_ref, am_ref, y_ref, s_ref):
    light, color = coefficients(ext_ref, cmap_ref, light_ref)
    odd_group = parity("depth")
    edge_before, edge_after = ends_inside("depth")

    def first(i, _):
        for row in (2 * i, 2 * i + 1):
            ends = [
                by_parity(odd_group, depth_first_ref[k, row], depth_second_ref[k, row])
                for k in range(2)
            ]
            z = binomial([ends[0][0], ends[1][0], cells(x_ref, row, 0), cells(x_ref, row, 1)])
            z += binomial([cells(x_ref, row, 6), cells(x_ref, row, 7), ends[0][1], ends[1][1]])
            z_ref[row, 0] = z[0] * edge_before
            z_ref[row, 1] = z[1]
            z_ref[row, 2] = z[2]
            z_ref[row, 3] = z[3] * edge_after
        return 0

    lax.fori_loop(0, ROWS // 2, first, 0, unroll=True)

    def second(i, _):
        row = PAIR * i + 1
        here = pl.ds(row, PAIR)
        s = smoothed(row_sums(z_ref[pl.ds(row - 1, PAIR + 2)]), 1.0 / 64.0)
        u, w = column_parts(s)
        for side in range(2):
            at = pl.ds(2 * side, 2)
            if side == 0:
                us = jnp.concatenate([u[:, 0:2], ui_ref[here, 0:2]], 1)
                ws = jnp.concatenate([w[:, 0:2], wi_ref[here, 0:2]], 1)
            else:
                us = jnp.concatenate([ui_ref[here, 2:4], u[:, 2:4]], 1)
                ws = jnp.concatenate([wi_ref[here, 2:4], w[:, 2:4]], 1)
            ap_ref[here, at], am_ref[here, at], y_ref[here, at] = gradient_parts(us, ws, light)
        s_ref[here, 0] = s[:, 1]
        s_ref[here, 1] = si_ref[here, 0]
        s_ref[here, 2] = si_ref[here, 5]
        s_ref[here, 3] = s[:, 2]
        return 0

    lax.fori_loop(0, (ROWS - 2) // PAIR, second, 0, unroll=True)

    def third(i, _):
        row = 2 * i + 2
        here = pl.ds(row, 2)
        facing = (ap_ref[pl.ds(row + 1, 2)] + am_ref[pl.ds(row - 1, 2)]) + y_ref[here]
        s = s_ref[here]
        front = shade(s[:, 0:2], facing[:, 0:2], None, *color)
        total = over(front, [mid_ref[c, here] for c in range(4)])
        total = shade(s[:, 2:4], facing[:, 2:4], total, *color)
        for c in range(4):
            part_ref[c, here] = total[c]
        return 0

    lax.fori_loop(0, (ROWS - 4) // 2, third, 0, unroll=True)

    def whole(inner, outer):
        return jnp.concatenate([outer[0:2], inner, outer[2:4]], 0)

    for i, row in enumerate((0, 1, ROWS - 1, ROWS - 2)):
        zk_ref[i] = whole(zi_ref[row], z_ref[row])
    facing_ref[0] = whole(api_ref[1], ap_ref[1])
    facing_ref[1] = whole(api_ref[2] + yi_ref[1], ap_ref[2] + y_ref[1])
    facing_ref[2] = whole(ami_ref[ROWS - 2], am_ref[ROWS - 2])
    facing_ref[3] = whole(ami_ref[ROWS - 3] + yi_ref[ROWS - 2], am_ref[ROWS - 3] + y_ref[ROWS - 2])
    for i, row in enumerate((1, ROWS - 2)):
        sk_ref[i, 0] = s_ref[row, 0]
        sk_ref[i, 1:7] = si_ref[row]
        sk_ref[i, 7] = s_ref[row, 3]


def render_rows(ext_ref, cmap_ref, light_ref, strip_first_ref, strip_second_ref, part_ref, zk_ref,
                facing_ref, sk_ref, out_ref, halo_ref, all_ref):
    light, color = coefficients(ext_ref, cmap_ref, light_ref)
    odd_strip = parity("strip")
    edge_before, edge_after = ends_inside("depth")
    edge_up, edge_down = ends_inside("strip")

    for half, ref in ((1 - odd_strip, strip_first_ref), (odd_strip, strip_second_ref)):
        for j in range(2):
            z = binomial([ref[slab, j] for slab in range(SLABS + 4)])
            z[0] = z[0] * edge_before
            z[-1] = z[-1] * edge_after
            for i, v in enumerate(z):
                halo_ref[3 * half + (1 - 2 * half) * j, i] = v

    def boundary(half, _):
        sign = 1.0 - 2.0 * half.astype(jnp.float32)
        inside = jnp.where(half == 0, edge_up, edge_down) * (1.0 / 64.0)
        outer, inner = halo_ref[2 * half], halo_ref[2 * half + 1]
        first, second = zk_ref[2 * half], zk_ref[2 * half + 1]
        mirrored = [light[0] * sign, light[1], light[2]]

        def row_parts(lower, middle, upper, factor):
            s = smoothed((lower + middle) + (middle + upper), factor)[None]
            return s[:, 1:-1], *gradient_parts(*column_parts(s), mirrored)

        def finish(row, s, facing):
            total = shade(s, facing, None, *color)
            for c in range(4):
                all_ref[pl.ds(pl.multiple_of((c * ROWS + row) * SUB, SUB), SUB), :] = total[c][0]

        _, _, beyond, _ = row_parts(outer, inner, first, inside)
        s, _, inward, own = row_parts(inner, first, second, 1.0 / 64.0)
        finish((ROWS - 1) * half, s, facing_ref[pl.ds(2 * half, 1)] + beyond + own)
        finish(1 + (ROWS - 3) * half, sk_ref[pl.ds(half, 1)], facing_ref[pl.ds(2 * half + 1, 1)] + inward)
        return 0

    lax.fori_loop(0, 2, boundary, 0)
    for c in range(4):
        for row in range(2, ROWS - 2):
            all_ref[(c * ROWS + row) * SUB : (c * ROWS + row + 1) * SUB, :] = part_ref[c, row]

    group = 1
    chunk = lax.broadcasted_iota(jnp.int32, (group, SUB, LANE), 2) // 16
    for start in range(0, SUB, group):
        v = []
        for g in range(8):
            tiles = [all_ref[pl.ds(g * 64 + start + t, SUB, stride=SUB), :] for t in range(group)]
            v.append(rolled(jnp.stack(tiles), 16 * g, 1) if g else jnp.stack(tiles))
        for bit in (1, 2, 4):
            v = [jnp.where((chunk & bit) != 0, v[(k + bit) % 8], v[k]) for k in range(8)]
        for m in range(8):
            block = rolled(v[-m % 8], LANE - 16 * m, 1) if m else v[0]
            for t in range(group):
                row = ((start + t) * 8 + m) * SUB
                out_ref[row : row + SUB, :] = block[t]


def composite(parts_ref, out_ref):
    is_clear = lax.broadcasted_iota(jnp.int32, (SUB, LANE), 1) >= 96
    count = parts_ref.shape[0] // SUB
    runs = 4
    through = [jnp.ones((SUB, LANE), jnp.float32)] * runs
    total = [jnp.zeros((SUB, LANE), jnp.float32)] * runs
    for step in range(count // runs):
        for run in range(runs):
            d = run * (count // runs) + step
            x = parts_ref[d * SUB : (d + 1) * SUB, :]
            total[run] = total[run] + through[run] * x
            m = jnp.where(is_clear, x, 1.0)
            m = m * pltpu.roll(m, 32, 1)
            m = m * pltpu.roll(m, 64, 1)
            through[run] = through[run] * m
    image, clear = total[0], through[0]
    for run in range(1, runs):
        image = image + clear * total[run]
        clear = clear * through[run]
    result = jnp.where(is_clear, 1.0 - clear, image)
    for i in range(8):
        moved = result if i == 0 else pltpu.roll(result, LANE - 16 * i, 1)
        out_ref[i * SUB : (i + 1) * SUB, :] = moved[:, 0:16]


def f32(*shape):
    return pltpu.VMEM(shape, jnp.float32)


def near(*arrays):
    return [pltpu.with_memory_space_constraint(a, pltpu.VMEM) for a in arrays]


def local(volume, extinction, color_map, light_direction):
    groups = lax.axis_size("depth")
    x = volume.reshape(ROWS, SLABS, SUB, LANE).transpose(0, 2, 1, 3).reshape(ROWS * 64, LANE)

    def swaps(count):
        out = []
        for start in range(2):
            half = [(i, i + 1) for i in range(start, count - 1, 2)]
            out.append(half + [(b, a) for a, b in half])
        return out

    def exchange(buffers, axis):
        out = []
        for v, p in zip(buffers, swaps(lax.axis_size(axis))):
            out.append(lax.ppermute(v, axis, p))
        return out

    packed = pl.pallas_call(
        pack_depth, in_specs=[VM], compiler_params=SMALL, out_specs=[VM, VM], name="pack_depth",
        out_shape=[f32(2, ROWS, SUB, LANE)] * 2,
    )(*near(x))
    near_depth = exchange(packed, "depth")

    params = (extinction, color_map, light_direction)

    def kernel(body, operands, shapes, scratch=()):
        return pl.pallas_call(
            body, in_specs=[SM] * 3 + [VM] * len(operands), out_specs=[VM] * len(shapes),
            compiler_params=SMALL, out_shape=[f32(*shape) for shape in shapes],
            scratch_shapes=[f32(*shape) for shape in scratch],
        )(*params, *near(*operands))

    four = (ROWS, 4, SUB, LANE)
    zi, ui, wi, api, ami, yi, si, mid = kernel(
        render_inner, (x, packed[0]),
        [(ROWS, 6, SUB, LANE)] + [four] * 5 + [(ROWS, 6, SUB, LANE), (4, ROWS, SUB, LANE)],
    )
    near_strip = exchange(
        pl.pallas_call(
            pack_strip, in_specs=[VM] * 4, compiler_params=SMALL, out_specs=[VM, VM], name="pack_strip",
            out_shape=[f32(SLABS + 4, 2, SUB, LANE)] * 2,
        )(*near(x, *near_depth, mid)),
        "strip",
    )
    kept = kernel(
        render_outer, (x, *near_depth, zi, ui, wi, api, ami, yi, si, mid),
        [(4, ROWS, SUB, LANE), (4, SLABS + 2, SUB, LANE), (4, SLABS, SUB, LANE), (2, SLABS, SUB, LANE)],
        [four] * 5,
    )
    (blocks,) = kernel(
        render_rows, (*near_strip, *kept),
        [(groups * SUB, LANE)], [(4, SLABS + 2, SUB, LANE), (4 * ROWS * SUB, LANE)],
    )
    layers = lax.all_to_all(
        blocks.reshape(groups, SUB, LANE), "depth", split_axis=0, concat_axis=0, tiled=True
    )
    image = pl.pallas_call(
        composite, in_specs=[VM], compiler_params=SMALL, out_specs=VM, name="composite",
        out_shape=jax.ShapeDtypeStruct((64, 16), jnp.float32),
    )(*near(layers.reshape(groups * SUB, LANE)))
    return image.reshape(4, 16, 16)


def solution(mesh):
    in_specs = (P("strip", "depth", None), P(), P(), P())
    out_specs = P(None, "strip", "depth")
    return jax.shard_map(local, mesh=mesh, in_specs=in_specs, out_specs=out_specs, check_vma=False)
```

```python
import jax
import jax.numpy as jnp
from jax import lax
from jax.experimental import pallas as pl
from jax.experimental.pallas import tpu as pltpu
from jax.sharding import PartitionSpec as P


ROWS, SLABS, SUB, LANE = 16, 8, 8, 128
PAIR = 2
VM = pl.BlockSpec(memory_space=pltpu.VMEM)
SM = pl.BlockSpec(memory_space=pltpu.SMEM)


SMALL = pltpu.CompilerParams(vmem_limit_bytes=4 << 20)


def cells(x_ref, row, slab):
    return x_ref[pl.ds(row * 64 + slab, SUB, stride=SLABS), :]


def parity(axis):
    return lax.axis_index(axis) % 2


def pack_depth(x_ref, first_ref, second_ref, sems):
    start = (SLABS - 2) * (1 - parity("depth"))
    copies = []
    for i, (ref, slab) in enumerate(((second_ref, (SLABS - 2) - start), (first_ref, start))):
        for k in range(2):
            copies.append(pltpu.make_async_copy(x_ref.at[:, slab + k], ref.at[k], sems.at[i, k]))
    for copy in copies:
        copy.start()
    for copy in copies:
        copy.wait()


def by_parity(odd, first, second):
    is_odd = odd == 1
    return jnp.where(is_odd, first, second), jnp.where(is_odd, second, first)


def pack_strip(x_ref, from_first_ref, from_second_ref, _, first_ref, second_ref):
    odd = parity("strip")
    group_odd = parity("depth")
    start = (ROWS - 2) * (1 - odd)
    for ref, row in ((first_ref, start), (second_ref, (ROWS - 2) - start)):
        for k in range(2):
            for j in range(2):
                before, after = by_parity(
                    group_odd, from_first_ref[j, row + k], from_second_ref[j, row + k]
                )
                ref[j, k] = before
                ref[SLABS + 2 + j, k] = after
            for slab in range(SLABS):
                ref[2 + slab, k] = cells(x_ref, row + k, slab)


def rolled(v, shift, axis):
    return pltpu.roll(v.reshape(-1, SUB, LANE), shift, axis + 1).reshape(v.shape)


def column_neighbours(v):
    lane = lax.broadcasted_iota(jnp.int32, v.shape, v.ndim - 1)
    sub = lax.broadcasted_iota(jnp.int32, v.shape, v.ndim - 2)
    a = rolled(v, 1, 1)
    prev = jnp.where(lane == 0, jnp.where(sub == 0, 0.0, rolled(a, 1, 0)), a)
    a = rolled(v, LANE - 1, 1)
    following = jnp.where(lane == LANE - 1, jnp.where(sub == SUB - 1, 0.0, rolled(a, SUB - 1, 0)), a)
    return prev, following


def log1p_unit(e):
    w = 1.0 + e
    return jnp.log(w) + (e - (w - 1.0))


def row_sums(z):
    e = z[:-1] + z[1:]
    return e[:-1] + e[1:]


def slab_sums(v):
    e = v[:, :-1] + v[:, 1:]
    return e[:, :-1] + e[:, 1:]


def smoothed(m, factor):
    prev, following = column_neighbours(m)
    return ((prev + following) + (m + m)) * factor


def column_parts(s):
    prev, following = column_neighbours(s)
    return (prev + following) + (s + s), following - prev


def gradient_parts(u, w, light):
    scale = 0.5 * 0.25 * 0.25
    y = (light[1] * scale) * (u[:, 2:] - u[:, :-2]) + (light[2] * scale) * slab_sums(w)
    p = (light[0] * scale) * slab_sums(u)
    return y + p, y - p, y + y


def shade(s, facing, front, ext, slopes, offsets):
    half = 0.5 - 0.35 / (1.0 + facing * facing)
    z = s + s
    soft = jnp.maximum(z, 0.0) + log1p_unit(jnp.exp(-jnp.abs(z)))
    clear = jnp.exp(-ext * soft)
    weight = (1.0 - clear) * half
    tones = [jnp.tanh(a * s + b) + 1.0 for a, b in zip(slopes, offsets)]
    total = front
    for k in range(s.shape[1]):
        if total is None:
            total = [weight[:, k] * t[:, k] for t in tones] + [clear[:, k]]
        else:
            here = weight[:, k] * total[3]
            total = [c + here * t[:, k] for c, t in zip(total, tones)] + [total[3] * clear[:, k]]
    return total


def over(front, back):
    through = front[3]
    return [f + through * c for f, c in zip(front[:3], back[:3])] + [through * back[3]]


def coefficients(ext_ref, cmap_ref, light_ref):
    light = [light_ref[i] for i in range(3)]
    slopes = [cmap_ref[c, 0] * 0.5 for c in range(3)]
    offsets = [cmap_ref[c, 1] * 0.5 for c in range(3)]
    return light, (ext_ref[0], slopes, offsets)


def ends_inside(axis):
    index, count = lax.axis_index(axis), lax.axis_size(axis)
    return jnp.where(index == 0, 0.0, 1.0), jnp.where(index == count - 1, 0.0, 1.0)


def binomial(v):
    e = [a + b for a, b in zip(v, v[1:])]
    return [a + b for a, b in zip(e, e[1:])]


def render_inner(ext_ref, cmap_ref, light_ref, x_ref, _, z_ref, u_ref, w_ref, ap_ref, am_ref, y_ref,
                 s_ref, mid_ref):
    light, color = coefficients(ext_ref, cmap_ref, light_ref)

    def first(i, _):
        for row in (2 * i, 2 * i + 1):
            z = binomial([cells(x_ref, row, slab) for slab in range(SLABS)])
            for i, v in enumerate(z):
                z_ref[row, i] = v
        return 0

    lax.fori_loop(0, ROWS // 2, first, 0, unroll=True)

    def second(i, _):
        row = PAIR * i + 1
        s = smoothed(row_sums(z_ref[pl.ds(row - 1, PAIR + 2)]), 1.0 / 64.0)
        u, w = column_parts(s)
        here = pl.ds(row, PAIR)
        for i, k in enumerate((0, 1, 4, 5)):
            u_ref[here, i] = u[:, k]
            w_ref[here, i] = w[:, k]
        ap_ref[here], am_ref[here], y_ref[here] = gradient_parts(u, w, light)
        s_ref[here] = s
        return 0

    lax.fori_loop(0, (ROWS - 2) // PAIR, second, 0, unroll=True)

    def third(i, _):
        row = 2 * i + 2
        here = pl.ds(row, 2)
        facing = (ap_ref[pl.ds(row + 1, 2)] + am_ref[pl.ds(row - 1, 2)]) + y_ref[here]
        total = shade(s_ref[here, 1:5], facing, None, *color)
        for c in range(4):
            mid_ref[c, here] = total[c]
        return 0

    lax.fori_loop(0, (ROWS - 4) // 2, third, 0, unroll=True)


def render_outer(ext_ref, cmap_ref, light_ref, x_ref, depth_first_ref, depth_second_ref, zi_ref,
                 ui_ref, wi_ref, api_ref, ami_ref, yi_ref, si_ref, mid_ref, part_ref, zk_ref,
                 facing_ref, sk_ref, z_ref, ap_ref, am_ref, y_ref, s_ref):
    light, color = coefficients(ext_ref, cmap_ref, light_ref)
    odd_group = parity("depth")
    edge_before, edge_after = ends_inside("depth")

    def first(i, _):
        for row in (2 * i, 2 * i + 1):
            ends = [
                by_parity(odd_group, depth_first_ref[k, row], depth_second_ref[k, row])
                for k in range(2)
            ]
            z = binomial([ends[0][0], ends[1][0], cells(x_ref, row, 0), cells(x_ref, row, 1)])
            z += binomial([cells(x_ref, row, 6), cells(x_ref, row, 7), ends[0][1], ends[1][1]])
            z_ref[row, 0] = z[0] * edge_before
            z_ref[row, 1] = z[1]
            z_ref[row, 2] = z[2]
            z_ref[row, 3] = z[3] * edge_after
        return 0

    lax.fori_loop(0, ROWS // 2, first, 0, unroll=True)

    def second(i, _):
        row = PAIR * i + 1
        here = pl.ds(row, PAIR)
        s = smoothed(row_sums(z_ref[pl.ds(row - 1, PAIR + 2)]), 1.0 / 64.0)
        u, w = column_parts(s)
        for side in range(2):
            at = pl.ds(2 * side, 2)
            if side == 0:
                us = jnp.concatenate([u[:, 0:2], ui_ref[here, 0:2]], 1)
                ws = jnp.concatenate([w[:, 0:2], wi_ref[here, 0:2]], 1)
            else:
                us = jnp.concatenate([ui_ref[here, 2:4], u[:, 2:4]], 1)
                ws = jnp.concatenate([wi_ref[here, 2:4], w[:, 2:4]], 1)
            ap_ref[here, at], am_ref[here, at], y_ref[here, at] = gradient_parts(us, ws, light)
        s_ref[here, 0] = s[:, 1]
        s_ref[here, 1] = si_ref[here, 0]
        s_ref[here, 2] = si_ref[here, 5]
        s_ref[here, 3] = s[:, 2]
        return 0

    lax.fori_loop(0, (ROWS - 2) // PAIR, second, 0, unroll=True)

    def third(i, _):
        row = 2 * i + 2
        here = pl.ds(row, 2)
        facing = (ap_ref[pl.ds(row + 1, 2)] + am_ref[pl.ds(row - 1, 2)]) + y_ref[here]
        s = s_ref[here]
        front = shade(s[:, 0:2], facing[:, 0:2], None, *color)
        total = over(front, [mid_ref[c, here] for c in range(4)])
        total = shade(s[:, 2:4], facing[:, 2:4], total, *color)
        for c in range(4):
            at = pl.multiple_of((c * ROWS + row) * SUB, SUB)
            part_ref[pl.ds(at, 2 * SUB), :] = total[c].reshape(2 * SUB, LANE)
        return 0

    lax.fori_loop(0, (ROWS - 4) // 2, third, 0, unroll=True)

    def whole(inner, outer):
        return jnp.concatenate([outer[0:2], inner, outer[2:4]], 0)

    for i, row in enumerate((0, 1, ROWS - 1, ROWS - 2)):
        zk_ref[i] = whole(zi_ref[row], z_ref[row])
    facing_ref[0] = whole(api_ref[1], ap_ref[1])
    facing_ref[1] = whole(api_ref[2] + yi_ref[1], ap_ref[2] + y_ref[1])
    facing_ref[2] = whole(ami_ref[ROWS - 2], am_ref[ROWS - 2])
    facing_ref[3] = whole(ami_ref[ROWS - 3] + yi_ref[ROWS - 2], am_ref[ROWS - 3] + y_ref[ROWS - 2])
    for i, row in enumerate((1, ROWS - 2)):
        sk_ref[i, 0] = s_ref[row, 0]
        sk_ref[i, 1:7] = si_ref[row]
        sk_ref[i, 7] = s_ref[row, 3]


def render_rows(ext_ref, cmap_ref, light_ref, strip_first_ref, strip_second_ref, _, zk_ref,
                facing_ref, sk_ref, out_ref, all_ref, halo_ref):
    light, color = coefficients(ext_ref, cmap_ref, light_ref)
    odd_strip = parity("strip")
    edge_before, edge_after = ends_inside("depth")
    edge_up, edge_down = ends_inside("strip")

    for half, ref in ((1 - odd_strip, strip_first_ref), (odd_strip, strip_second_ref)):
        for j in range(2):
            z = binomial([ref[slab, j] for slab in range(SLABS + 4)])
            z[0] = z[0] * edge_before
            z[-1] = z[-1] * edge_after
            for i, v in enumerate(z):
                halo_ref[3 * half + (1 - 2 * half) * j, i] = v

    def boundary(half, _):
        sign = 1.0 - 2.0 * half.astype(jnp.float32)
        inside = jnp.where(half == 0, edge_up, edge_down) * (1.0 / 64.0)
        outer, inner = halo_ref[2 * half], halo_ref[2 * half + 1]
        first, second = zk_ref[2 * half], zk_ref[2 * half + 1]
        mirrored = [light[0] * sign, light[1], light[2]]

        def row_parts(lower, middle, upper, factor):
            s = smoothed((lower + middle) + (middle + upper), factor)[None]
            return s[:, 1:-1], *gradient_parts(*column_parts(s), mirrored)

        def finish(row, s, facing):
            total = shade(s, facing, None, *color)
            for c in range(4):
                all_ref[pl.ds(pl.multiple_of((c * ROWS + row) * SUB, SUB), SUB), :] = total[c][0]

        _, _, beyond, _ = row_parts(outer, inner, first, inside)
        s, _, inward, own = row_parts(inner, first, second, 1.0 / 64.0)
        finish((ROWS - 1) * half, s, facing_ref[pl.ds(2 * half, 1)] + beyond + own)
        finish(1 + (ROWS - 3) * half, sk_ref[pl.ds(half, 1)], facing_ref[pl.ds(2 * half + 1, 1)] + inward)
        return 0

    lax.fori_loop(0, 2, boundary, 0, unroll=True)
    group = 1
    chunk = lax.broadcasted_iota(jnp.int32, (group, SUB, LANE), 2) // 16
    for start in range(0, SUB, group):
        v = []
        for g in range(8):
            tiles = [all_ref[pl.ds(g * 64 + start + t, SUB, stride=SUB), :] for t in range(group)]
            v.append(rolled(jnp.stack(tiles), 16 * g, 1) if g else jnp.stack(tiles))
        for bit in (1, 2, 4):
            v = [jnp.where((chunk & bit) != 0, v[(k + bit) % 8], v[k]) for k in range(8)]
        for m in range(8):
            block = rolled(v[-m % 8], LANE - 16 * m, 1) if m else v[0]
            for t in range(group):
                row = ((start + t) * 8 + m) * SUB
                out_ref[row : row + SUB, :] = block[t]


def composite(parts_ref, out_ref):
    is_clear = lax.broadcasted_iota(jnp.int32, (SUB, LANE), 1) >= 96
    count = parts_ref.shape[0] // SUB
    runs = 4
    through = [jnp.ones((SUB, LANE), jnp.float32)] * runs
    total = [jnp.zeros((SUB, LANE), jnp.float32)] * runs
    for step in range(count // runs):
        for run in range(runs):
            d = run * (count // runs) + step
            x = parts_ref[d * SUB : (d + 1) * SUB, :]
            total[run] = total[run] + through[run] * x
            m = jnp.where(is_clear, x, 1.0)
            m = m * pltpu.roll(m, 32, 1)
            m = m * pltpu.roll(m, 64, 1)
            through[run] = through[run] * m
    image, clear = total[0], through[0]
    for run in range(1, runs):
        image = image + clear * total[run]
        clear = clear * through[run]
    result = jnp.where(is_clear, 1.0 - clear, image)
    for i in range(8):
        moved = result if i == 0 else pltpu.roll(result, LANE - 16 * i, 1)
        out_ref[i * SUB : (i + 1) * SUB, :] = moved[:, 0:16]


def f32(*shape):
    return pltpu.VMEM(shape, jnp.float32)


def near(*arrays):
    return [pltpu.with_memory_space_constraint(a, pltpu.VMEM) for a in arrays]


def local(volume, extinction, color_map, light_direction):
    groups = lax.axis_size("depth")
    x = volume.reshape(ROWS, SLABS, SUB, LANE).transpose(0, 2, 1, 3).reshape(ROWS * 64, LANE)

    def swaps(count):
        out = []
        for start in range(2):
            half = [(i, i + 1) for i in range(start, count - 1, 2)]
            out.append(half + [(b, a) for a, b in half])
        return out

    def exchange(buffers, axis):
        out = []
        for v, p in zip(buffers, swaps(lax.axis_size(axis))):
            out.append(lax.ppermute(v, axis, p))
        return out

    packed = pl.pallas_call(
        pack_depth, in_specs=[pl.BlockSpec(memory_space=pltpu.HBM)], out_specs=[VM, VM],
        compiler_params=SMALL, name="pack_depth",
        out_shape=[f32(2, ROWS * SUB, 1, LANE)] * 2,
        scratch_shapes=[pltpu.SemaphoreType.DMA((2, 2))],
    )(pltpu.with_memory_space_constraint(x.reshape(ROWS * SUB, SLABS, 1, LANE), pltpu.HBM))
    packed = [v.reshape(2, ROWS, SUB, LANE) for v in packed]
    near_depth = exchange(packed, "depth")

    params = (extinction, color_map, light_direction)

    def kernel(body, operands, shapes, scratch=(), aliases={}):
        return pl.pallas_call(
            body, in_specs=[SM] * 3 + [VM] * len(operands), out_specs=[VM] * len(shapes),
            compiler_params=SMALL, input_output_aliases=aliases, out_shape=[f32(*shape) for shape in shapes],
            scratch_shapes=[f32(*shape) for shape in scratch],
        )(*params, *near(*operands))

    four = (ROWS, 4, SUB, LANE)
    zi, ui, wi, api, ami, yi, si, mid = kernel(
        render_inner, (x, packed[0]),
        [(ROWS, 6, SUB, LANE)] + [four] * 5 + [(ROWS, 6, SUB, LANE), (4, ROWS, SUB, LANE)],
    )
    near_strip = exchange(
        pl.pallas_call(
            pack_strip, in_specs=[VM] * 4, compiler_params=SMALL, out_specs=[VM, VM], name="pack_strip",
            out_shape=[f32(SLABS + 4, 2, SUB, LANE)] * 2,
        )(*near(x, *near_depth, mid)),
        "strip",
    )
    kept = kernel(
        render_outer, (x, *near_depth, zi, ui, wi, api, ami, yi, si, mid),
        [(4 * ROWS * SUB, LANE), (4, SLABS + 2, SUB, LANE), (4, SLABS, SUB, LANE), (2, SLABS, SUB, LANE)],
        [four] * 5,
    )
    blocks, _ = kernel(
        render_rows, (*near_strip, *kept), [(groups * SUB, LANE), (4 * ROWS * SUB, LANE)],
        [(4, SLABS + 2, SUB, LANE)], {5: 1},
    )
    layers = lax.all_to_all(
        blocks.reshape(groups, SUB, LANE), "depth", split_axis=0, concat_axis=0, tiled=True
    )
    image = pl.pallas_call(
        composite, in_specs=[VM], compiler_params=SMALL, out_specs=VM, name="composite",
        out_shape=jax.ShapeDtypeStruct((64, 16), jnp.float32),
    )(*near(layers.reshape(groups * SUB, LANE)))
    return image.reshape(4, 16, 16)


def solution(mesh):
    in_specs = (P("strip", "depth", None), P(), P(), P())
    out_specs = P(None, "strip", "depth")
    return jax.shard_map(local, mesh=mesh, in_specs=in_specs, out_specs=out_specs, check_vma=False)
```

```python
import jax
import jax.numpy as jnp
from jax import lax
from jax.experimental import pallas as pl
from jax.experimental.pallas import tpu as pltpu
from jax.sharding import PartitionSpec as P


ROWS, SLABS, SUB, LANE = 16, 8, 8, 128
PAIR = 2
VM = pl.BlockSpec(memory_space=pltpu.VMEM)
SM = pl.BlockSpec(memory_space=pltpu.SMEM)


SMALL = pltpu.CompilerParams(vmem_limit_bytes=4 << 20)


def cells(x_ref, row, slab):
    return x_ref[pl.ds(row * 64 + slab, SUB, stride=SLABS), :]


def parity(axis):
    return lax.axis_index(axis) % 2


def pack_depth(x_ref, first_ref, second_ref, sems):
    start = (SLABS - 2) * (1 - parity("depth"))
    copies = []
    for i, (ref, slab) in enumerate(((second_ref, (SLABS - 2) - start), (first_ref, start))):
        for k in range(2):
            copies.append(pltpu.make_async_copy(x_ref.at[:, slab + k], ref.at[k], sems.at[i, k]))
    for copy in copies:
        copy.start()
    for copy in copies:
        copy.wait()


def by_parity(odd, first, second):
    is_odd = odd == 1
    return jnp.where(is_odd, first, second), jnp.where(is_odd, second, first)


def pack_strip(x_ref, from_first_ref, from_second_ref, _, first_ref, second_ref):
    odd = parity("strip")
    group_odd = parity("depth")
    start = (ROWS - 2) * (1 - odd)
    for ref, row in ((first_ref, start), (second_ref, (ROWS - 2) - start)):
        for k in range(2):
            for j in range(2):
                before, after = by_parity(
                    group_odd, from_first_ref[j, row + k], from_second_ref[j, row + k]
                )
                ref[j, k] = before
                ref[SLABS + 2 + j, k] = after
            for slab in range(SLABS):
                ref[2 + slab, k] = cells(x_ref, row + k, slab)


def rolled(v, shift, axis):
    return pltpu.roll(v.reshape(-1, SUB, LANE), shift, axis + 1).reshape(v.shape)


def column_neighbours(v):
    lane = lax.broadcasted_iota(jnp.int32, v.shape, v.ndim - 1)
    sub = lax.broadcasted_iota(jnp.int32, v.shape, v.ndim - 2)
    a = rolled(v, 1, 1)
    prev = jnp.where(lane == 0, jnp.where(sub == 0, 0.0, rolled(a, 1, 0)), a)
    a = rolled(v, LANE - 1, 1)
    following = jnp.where(lane == LANE - 1, jnp.where(sub == SUB - 1, 0.0, rolled(a, SUB - 1, 0)), a)
    return prev, following


def log1p_unit(e):
    w = 1.0 + e
    return jnp.log(w) + (e - (w - 1.0))


def row_sums(z):
    e = z[:-1] + z[1:]
    return e[:-1] + e[1:]


def slab_sums(v):
    e = v[:, :-1] + v[:, 1:]
    return e[:, :-1] + e[:, 1:]


def smoothed(m, factor):
    prev, following = column_neighbours(m)
    return ((prev + following) + (m + m)) * factor


def column_parts(s):
    prev, following = column_neighbours(s)
    return (prev + following) + (s + s), following - prev


def gradient_parts(u, w, light):
    scale = 0.5 * 0.25 * 0.25
    y = (light[1] * scale) * (u[:, 2:] - u[:, :-2]) + (light[2] * scale) * slab_sums(w)
    p = (light[0] * scale) * slab_sums(u)
    return y + p, y - p, y + y


def matter(s, ext, slopes, offsets):
    z = s + s
    soft = jnp.maximum(z, 0.0) + log1p_unit(jnp.exp(-jnp.abs(z)))
    return jnp.exp(-ext * soft), [jnp.tanh(a * s + b) + 1.0 for a, b in zip(slopes, offsets)]


def shade(cells_matter, facing, front):
    clear, tones = cells_matter
    weight = (1.0 - clear) * (0.5 - 0.35 / (1.0 + facing * facing))
    total = front
    for k in range(facing.shape[1]):
        if total is None:
            total = [weight[:, k] * t[:, k] for t in tones] + [clear[:, k]]
        else:
            here = weight[:, k] * total[3]
            total = [c + here * t[:, k] for c, t in zip(total, tones)] + [total[3] * clear[:, k]]
    return total


def over(front, back):
    through = front[3]
    return [f + through * c for f, c in zip(front[:3], back[:3])] + [through * back[3]]


def turned(v, channel, half):
    turn = 16 * (2 * channel + half)
    return rolled(v, turn, 1) if turn else v


def coefficients(ext_ref, cmap_ref, light_ref):
    light = [light_ref[i] for i in range(3)]
    slopes = [cmap_ref[c, 0] * 0.5 for c in range(3)]
    offsets = [cmap_ref[c, 1] * 0.5 for c in range(3)]
    return light, (ext_ref[0], slopes, offsets)


def ends_inside(axis):
    index, count = lax.axis_index(axis), lax.axis_size(axis)
    return jnp.where(index == 0, 0.0, 1.0), jnp.where(index == count - 1, 0.0, 1.0)


def binomial(v):
    e = [a + b for a, b in zip(v, v[1:])]
    return [a + b for a, b in zip(e, e[1:])]


def render_inner(ext_ref, cmap_ref, light_ref, x_ref, _, z_ref, u_ref, w_ref, ap_ref, am_ref, y_ref,
                 s_ref, mid_ref, sides_ref, ends_ref):
    light, color = coefficients(ext_ref, cmap_ref, light_ref)

    def first(i, _):
        for row in (2 * i, 2 * i + 1):
            z = binomial([cells(x_ref, row, slab) for slab in range(SLABS)])
            for i, v in enumerate(z):
                z_ref[row, i] = v
        return 0

    lax.fori_loop(0, ROWS // 2, first, 0, unroll=True)

    def second(i, _):
        row = PAIR * i + 1
        s = smoothed(row_sums(z_ref[pl.ds(row - 1, PAIR + 2)]), 1.0 / 64.0)
        u, w = column_parts(s)
        here = pl.ds(row, PAIR)
        for i, k in enumerate((0, 1, 4, 5)):
            u_ref[here, i] = u[:, k]
            w_ref[here, i] = w[:, k]
        ap_ref[here], am_ref[here], y_ref[here] = gradient_parts(u, w, light)
        s_ref[here] = s
        return 0

    lax.fori_loop(0, (ROWS - 2) // PAIR, second, 0, unroll=True)

    def third(i, _):
        row = 2 * i + 2
        here = pl.ds(row, 2)
        facing = (ap_ref[pl.ds(row + 1, 2)] + am_ref[pl.ds(row - 1, 2)]) + y_ref[here]
        clear, tones = matter(s_ref[here], *color)
        total = shade((clear[:, 1:5], [t[:, 1:5] for t in tones]), facing, None)
        for c in range(4):
            mid_ref[c, here] = total[c]
        for c, v in enumerate((*tones, clear)):
            sides_ref[c, here, 0] = v[:, 0]
            sides_ref[c, here, 1] = v[:, 5]
        return 0

    lax.fori_loop(0, (ROWS - 4) // 2, third, 0, unroll=True)
    for i, row in enumerate((1, ROWS - 2)):
        clear, tones = matter(s_ref[row : row + 1], *color)
        for c, v in enumerate((*tones, clear)):
            ends_ref[c, i] = v[0]


def render_outer(ext_ref, cmap_ref, light_ref, x_ref, depth_first_ref, depth_second_ref, zi_ref,
                 ui_ref, wi_ref, api_ref, ami_ref, yi_ref, mid_ref, sides_ref, ends_ref,
                 part_ref, zk_ref, facing_ref, known_ref, z_ref, ap_ref, am_ref, y_ref, s_ref):
    light, color = coefficients(ext_ref, cmap_ref, light_ref)
    odd_group = parity("depth")
    edge_before, edge_after = ends_inside("depth")

    def first(i, _):
        for row in (2 * i, 2 * i + 1):
            ends = [
                by_parity(odd_group, depth_first_ref[k, row], depth_second_ref[k, row])
                for k in range(2)
            ]
            z = binomial([ends[0][0], ends[1][0], cells(x_ref, row, 0), cells(x_ref, row, 1)])
            z += binomial([cells(x_ref, row, 6), cells(x_ref, row, 7), ends[0][1], ends[1][1]])
            z_ref[row, 0] = z[0] * edge_before
            z_ref[row, 1] = z[1]
            z_ref[row, 2] = z[2]
            z_ref[row, 3] = z[3] * edge_after
        return 0

    lax.fori_loop(0, ROWS // 2, first, 0, unroll=True)

    def second(i, _):
        row = PAIR * i + 1
        here = pl.ds(row, PAIR)
        s = smoothed(row_sums(z_ref[pl.ds(row - 1, PAIR + 2)]), 1.0 / 64.0)
        u, w = column_parts(s)
        for side in range(2):
            at = pl.ds(2 * side, 2)
            if side == 0:
                us = jnp.concatenate([u[:, 0:2], ui_ref[here, 0:2]], 1)
                ws = jnp.concatenate([w[:, 0:2], wi_ref[here, 0:2]], 1)
            else:
                us = jnp.concatenate([ui_ref[here, 2:4], u[:, 2:4]], 1)
                ws = jnp.concatenate([wi_ref[here, 2:4], w[:, 2:4]], 1)
            ap_ref[here, at], am_ref[here, at], y_ref[here, at] = gradient_parts(us, ws, light)
        s_ref[here] = s[:, 1:3]
        return 0

    lax.fori_loop(0, (ROWS - 2) // PAIR, second, 0, unroll=True)

    def third(i):
        row = 2 * i + 2
        here = pl.ds(row, 2)
        facing = (ap_ref[pl.ds(row + 1, 2)] + am_ref[pl.ds(row - 1, 2)]) + y_ref[here]
        clear, tones = matter(s_ref[here], *color)
        own, kept = (*tones, clear), [sides_ref[c, here] for c in range(4)]
        front = [jnp.concatenate([a[:, :1], b[:, :1]], 1) for a, b in zip(own, kept)]
        back = [jnp.concatenate([b[:, 1:], a[:, 1:]], 1) for a, b in zip(own, kept)]
        total = shade((front[3], front[:3]), facing[:, 0:2], None)
        total = over(total, [mid_ref[c, here] for c in range(4)])
        total = shade((back[3], back[:3]), facing[:, 2:4], total)
        for c in range(4):
            at = pl.multiple_of((c * ROWS + row) * SUB, SUB)
            part_ref[pl.ds(at, 2 * SUB), :] = turned(total[c], c, i // 3).reshape(2 * SUB, LANE)
        return 0

    for i in range((ROWS - 4) // 2):
        third(i)

    def whole(inner, outer):
        return jnp.concatenate([outer[0:2], inner, outer[2:4]], 0)

    for i, row in enumerate((0, 1, ROWS - 1, ROWS - 2)):
        zk_ref[i] = whole(zi_ref[row], z_ref[row])
    facing_ref[0] = whole(api_ref[1], ap_ref[1])
    facing_ref[1] = whole(api_ref[2] + yi_ref[1], ap_ref[2] + y_ref[1])
    facing_ref[2] = whole(ami_ref[ROWS - 2], am_ref[ROWS - 2])
    facing_ref[3] = whole(ami_ref[ROWS - 3] + yi_ref[ROWS - 2], am_ref[ROWS - 3] + y_ref[ROWS - 2])
    for i, row in enumerate((1, ROWS - 2)):
        clear, tones = matter(s_ref[row : row + 1], *color)
        for c, v in enumerate((*tones, clear)):
            known_ref[c, i, 0] = v[0, 0]
            known_ref[c, i, 1:7] = ends_ref[c, i]
            known_ref[c, i, 7] = v[0, 1]


def render_rows(ext_ref, cmap_ref, light_ref, strip_first_ref, strip_second_ref, _, zk_ref,
                facing_ref, known_ref, out_ref, all_ref, halo_ref):
    light, color = coefficients(ext_ref, cmap_ref, light_ref)
    odd_strip = parity("strip")
    edge_before, edge_after = ends_inside("depth")
    edge_up, edge_down = ends_inside("strip")

    for half, ref in ((1 - odd_strip, strip_first_ref), (odd_strip, strip_second_ref)):
        for j in range(2):
            z = binomial([ref[slab, j] for slab in range(SLABS + 4)])
            z[0] = z[0] * edge_before
            z[-1] = z[-1] * edge_after
            for i, v in enumerate(z):
                halo_ref[3 * half + (1 - 2 * half) * j, i] = v

    for half in range(2):
        sign = 1.0 - 2.0 * half
        inside = (edge_down if half else edge_up) * (1.0 / 64.0)
        outer, inner = halo_ref[2 * half], halo_ref[2 * half + 1]
        first, second = zk_ref[2 * half], zk_ref[2 * half + 1]
        mirrored = [light[0] * sign, light[1], light[2]]

        def row_parts(lower, middle, upper, factor):
            s = smoothed((lower + middle) + (middle + upper), factor)[None]
            return s[:, 1:-1], *gradient_parts(*column_parts(s), mirrored)

        def finish(row, found, facing):
            total = shade(found, facing, None)
            for c in range(4):
                at = (c * ROWS + row) * SUB
                all_ref[at : at + SUB, :] = turned(total[c], c, half)[0]

        _, _, beyond, _ = row_parts(outer, inner, first, inside)
        s, _, inward, own = row_parts(inner, first, second, 1.0 / 64.0)
        finish((ROWS - 1) * half, matter(s, *color), facing_ref[pl.ds(2 * half, 1)] + beyond + own)
        known = [known_ref[c, half : half + 1] for c in range(4)]
        finish(1 + (ROWS - 3) * half, (known[3], known[:3]), facing_ref[pl.ds(2 * half + 1, 1)] + inward)

    chunk = lax.broadcasted_iota(jnp.int32, (SUB, LANE), 1) // 16
    for tile in range(SUB):
        v = [all_ref[pl.ds(g * 64 + tile, SUB, stride=SUB), :] for g in range(8)]
        for bit in (1, 2, 4):
            v = [jnp.where((chunk & bit) != 0, v[(k + bit) % 8], v[k]) for k in range(8)]
        for m in range(8):
            row = (tile * 8 + m) * SUB
            out_ref[row : row + SUB, :] = rolled(v[-m % 8], LANE - 16 * m, 1) if m else v[0]


def composite(parts_ref, out_ref):
    is_clear = lax.broadcasted_iota(jnp.int32, (SUB, LANE), 1) >= 96
    count = parts_ref.shape[0] // SUB
    runs = 4
    through = [jnp.ones((SUB, LANE), jnp.float32)] * runs
    total = [jnp.zeros((SUB, LANE), jnp.float32)] * runs
    for step in range(count // runs):
        for run in range(runs):
            d = run * (count // runs) + step
            x = parts_ref[d * SUB : (d + 1) * SUB, :]
            total[run] = total[run] + through[run] * x
            m = jnp.where(is_clear, x, 1.0)
            m = m * pltpu.roll(m, 32, 1)
            m = m * pltpu.roll(m, 64, 1)
            through[run] = through[run] * m
    image, clear = total[0], through[0]
    for run in range(1, runs):
        image = image + clear * total[run]
        clear = clear * through[run]
    result = jnp.where(is_clear, 1.0 - clear, image)
    for i in range(8):
        moved = result if i == 0 else pltpu.roll(result, LANE - 16 * i, 1)
        out_ref[i * SUB : (i + 1) * SUB, :] = moved[:, 0:16]


def f32(*shape):
    return pltpu.VMEM(shape, jnp.float32)


def near(*arrays):
    return [pltpu.with_memory_space_constraint(a, pltpu.VMEM) for a in arrays]


def local(volume, extinction, color_map, light_direction):
    groups = lax.axis_size("depth")
    x = volume.reshape(ROWS, SLABS, SUB, LANE).transpose(0, 2, 1, 3).reshape(ROWS * 64, LANE)

    def swaps(count):
        out = []
        for start in range(2):
            half = [(i, i + 1) for i in range(start, count - 1, 2)]
            out.append(half + [(b, a) for a, b in half])
        return out

    def exchange(buffers, axis):
        out = []
        for v, p in zip(buffers, swaps(lax.axis_size(axis))):
            out.append(lax.ppermute(v, axis, p))
        return out

    packed = pl.pallas_call(
        pack_depth, in_specs=[pl.BlockSpec(memory_space=pltpu.HBM)], out_specs=[VM, VM],
        compiler_params=SMALL, name="pack_depth",
        out_shape=[f32(2, ROWS * SUB, 1, LANE)] * 2,
        scratch_shapes=[pltpu.SemaphoreType.DMA((2, 2))],
    )(pltpu.with_memory_space_constraint(x.reshape(ROWS * SUB, SLABS, 1, LANE), pltpu.HBM))
    packed = [v.reshape(2, ROWS, SUB, LANE) for v in packed]
    near_depth = exchange(packed, "depth")

    params = (extinction, color_map, light_direction)

    def kernel(body, operands, shapes, scratch=(), aliases={}):
        return pl.pallas_call(
            body, in_specs=[SM] * 3 + [VM] * len(operands), out_specs=[VM] * len(shapes),
            compiler_params=SMALL, input_output_aliases=aliases, out_shape=[f32(*shape) for shape in shapes],
            scratch_shapes=[f32(*shape) for shape in scratch],
        )(*params, *near(*operands))

    four = (ROWS, 4, SUB, LANE)
    zi, ui, wi, api, ami, yi, _, mid, sides, ends = kernel(
        render_inner, (x, packed[0]),
        [(ROWS, 6, SUB, LANE)] + [four] * 5
        + [(ROWS, 6, SUB, LANE), (4, ROWS, SUB, LANE), (4, ROWS, 2, SUB, LANE), (4, 2, 6, SUB, LANE)],
    )
    near_strip = exchange(
        pl.pallas_call(
            pack_strip, in_specs=[VM] * 4, compiler_params=SMALL, out_specs=[VM, VM], name="pack_strip",
            out_shape=[f32(SLABS + 4, 2, SUB, LANE)] * 2,
        )(*near(x, *near_depth, mid)),
        "strip",
    )
    kept = kernel(
        render_outer, (x, *near_depth, zi, ui, wi, api, ami, yi, mid, sides, ends),
        [(4 * ROWS * SUB, LANE), (4, SLABS + 2, SUB, LANE), (4, SLABS, SUB, LANE), (4, 2, SLABS, SUB, LANE)],
        [four] * 4 + [(ROWS, 2, SUB, LANE)],
    )
    blocks, _ = kernel(
        render_rows, (*near_strip, *kept), [(groups * SUB, LANE), (4 * ROWS * SUB, LANE)],
        [(4, SLABS + 2, SUB, LANE)], {5: 1},
    )
    layers = lax.all_to_all(
        blocks.reshape(groups, SUB, LANE), "depth", split_axis=0, concat_axis=0, tiled=True
    )
    image = pl.pallas_call(
        composite, in_specs=[VM], compiler_params=SMALL, out_specs=VM, name="composite",
        out_shape=jax.ShapeDtypeStruct((64, 16), jnp.float32),
    )(*near(layers.reshape(groups * SUB, LANE)))
    return image.reshape(4, 16, 16)


def solution(mesh):
    in_specs = (P("strip", "depth", None), P(), P(), P())
    out_specs = P(None, "strip", "depth")
    return jax.shard_map(local, mesh=mesh, in_specs=in_specs, out_specs=out_specs, check_vma=False)
```

```python
import jax
import jax.numpy as jnp
from jax import lax
from jax.experimental import pallas as pl
from jax.experimental.pallas import tpu as pltpu
from jax.sharding import PartitionSpec as P


ROWS, SLABS, SUB, LANE = 16, 8, 8, 128
PAIR = 2
VM = pl.BlockSpec(memory_space=pltpu.VMEM)
SM = pl.BlockSpec(memory_space=pltpu.SMEM)


SMALL = pltpu.CompilerParams(vmem_limit_bytes=4 << 20)


def cells(x_ref, row, slab):
    return x_ref[pl.ds(row * 64 + slab, SUB, stride=SLABS), :]


def parity(axis):
    return lax.axis_index(axis) % 2


def pack_depth(x_ref, first_ref, second_ref, sems):
    start = (SLABS - 2) * (1 - parity("depth"))
    copies = []
    for i, (ref, slab) in enumerate(((second_ref, (SLABS - 2) - start), (first_ref, start))):
        for k in range(2):
            copies.append(pltpu.make_async_copy(x_ref.at[:, slab + k], ref.at[k], sems.at[i, k]))
    for copy in copies:
        copy.start()
    for copy in copies:
        copy.wait()


def by_parity(odd, first, second):
    is_odd = odd == 1
    return jnp.where(is_odd, first, second), jnp.where(is_odd, second, first)


def pack_strip(x_ref, from_first_ref, from_second_ref, _, first_ref, second_ref):
    odd = parity("strip")
    group_odd = parity("depth")
    start = (ROWS - 2) * (1 - odd)
    for ref, row in ((first_ref, start), (second_ref, (ROWS - 2) - start)):
        for k in range(2):
            for j in range(2):
                before, after = by_parity(
                    group_odd, from_first_ref[j, row + k], from_second_ref[j, row + k]
                )
                ref[j, k] = before
                ref[SLABS + 2 + j, k] = after
            for slab in range(SLABS):
                ref[2 + slab, k] = cells(x_ref, row + k, slab)


def rolled(v, shift, axis):
    return pltpu.roll(v.reshape(-1, SUB, LANE), shift, axis + 1).reshape(v.shape)


def column_neighbours(v):
    lane = lax.broadcasted_iota(jnp.int32, v.shape, v.ndim - 1)
    sub = lax.broadcasted_iota(jnp.int32, v.shape, v.ndim - 2)
    a = rolled(v, 1, 1)
    prev = jnp.where(lane == 0, jnp.where(sub == 0, 0.0, rolled(a, 1, 0)), a)
    a = rolled(v, LANE - 1, 1)
    following = jnp.where(lane == LANE - 1, jnp.where(sub == SUB - 1, 0.0, rolled(a, SUB - 1, 0)), a)
    return prev, following


def log1p_unit(e):
    w = 1.0 + e
    return jnp.log(w) + (e - (w - 1.0))


def row_sums(z):
    e = z[:-1] + z[1:]
    return e[:-1] + e[1:]


def slab_sums(v):
    e = v[:, :-1] + v[:, 1:]
    return e[:, :-1] + e[:, 1:]


def smoothed(m, factor):
    prev, following = column_neighbours(m)
    return ((prev + following) + (m + m)) * factor


def column_parts(s):
    prev, following = column_neighbours(s)
    return (prev + following) + (s + s), following - prev


def gradient_parts(u, w, light):
    scale = 0.5 * 0.25 * 0.25
    y = (light[1] * scale) * (u[:, 2:] - u[:, :-2]) + (light[2] * scale) * slab_sums(w)
    p = (light[0] * scale) * slab_sums(u)
    return y + p, y - p, y + y


def matter(s, ext, slopes, offsets):
    z = s + s
    soft = jnp.maximum(z, 0.0) + log1p_unit(jnp.exp(-jnp.abs(z)))
    return jnp.exp(-ext * soft), [jnp.tanh(a * s + b) + 1.0 for a, b in zip(slopes, offsets)]


def shade(cells_matter, facing, front):
    clear, tones = cells_matter
    weight = (1.0 - clear) * (0.5 - 0.35 / (1.0 + facing * facing))
    total = front
    for k in range(facing.shape[1]):
        if total is None:
            total = [weight[:, k] * t[:, k] for t in tones] + [clear[:, k]]
        else:
            here = weight[:, k] * total[3]
            total = [c + here * t[:, k] for c, t in zip(total, tones)] + [total[3] * clear[:, k]]
    return total


def over(front, back):
    through = front[3]
    return [f + through * c for f, c in zip(front[:3], back[:3])] + [through * back[3]]


def turned(v, channel, half):
    turn = 16 * (2 * channel + half)
    return rolled(v, turn, 1) if turn else v


def coefficients(splat_ref):
    light, slopes, offsets = ([splat_ref[3 * i + c] for c in range(3)] for i in range(3))
    return light, (splat_ref[9], slopes, offsets)


def ends_inside(axis):
    index, count = lax.axis_index(axis), lax.axis_size(axis)
    return jnp.where(index == 0, 0.0, 1.0), jnp.where(index == count - 1, 0.0, 1.0)


def binomial(v):
    e = [a + b for a, b in zip(v, v[1:])]
    return [a + b for a, b in zip(e, e[1:])]


def render_inner(ext_ref, cmap_ref, light_ref, x_ref, _, splat_ref, z_ref, u_ref, w_ref, ap_ref, am_ref, y_ref,
                 s_ref, mid_ref, sides_ref, ends_ref):
    values = [light_ref[c] for c in range(3)]
    values += [cmap_ref[i, c] * 0.5 for i in range(2) for c in range(3)]
    for i, v in enumerate((*values, ext_ref[0])):
        splat_ref[i] = jnp.full((SUB, LANE), v, jnp.float32)
    light, color = values[:3], (ext_ref[0], values[3:6], values[6:9])

    def first(i, _):
        for row in (2 * i, 2 * i + 1):
            z = binomial([cells(x_ref, row, slab) for slab in range(SLABS)])
            for i, v in enumerate(z):
                z_ref[row, i] = v
        return 0

    lax.fori_loop(0, ROWS // 2, first, 0, unroll=True)

    def second(i, _):
        row = PAIR * i + 1
        s = smoothed(row_sums(z_ref[pl.ds(row - 1, PAIR + 2)]), 1.0 / 64.0)
        u, w = column_parts(s)
        here = pl.ds(row, PAIR)
        for i, k in enumerate((0, 1, 4, 5)):
            u_ref[here, i] = u[:, k]
            w_ref[here, i] = w[:, k]
        ap_ref[here], am_ref[here], y_ref[here] = gradient_parts(u, w, light)
        s_ref[here] = s
        return 0

    lax.fori_loop(0, (ROWS - 2) // PAIR, second, 0, unroll=True)

    def third(i, _):
        row = 2 * i + 2
        here = pl.ds(row, 2)
        facing = (ap_ref[pl.ds(row + 1, 2)] + am_ref[pl.ds(row - 1, 2)]) + y_ref[here]
        clear, tones = matter(s_ref[here], *color)
        total = shade((clear[:, 1:5], [t[:, 1:5] for t in tones]), facing, None)
        for c in range(4):
            mid_ref[c, here] = total[c]
        for c, v in enumerate((*tones, clear)):
            sides_ref[c, here, 0] = v[:, 0]
            sides_ref[c, here, 1] = v[:, 5]
        return 0

    lax.fori_loop(0, (ROWS - 4) // 2, third, 0, unroll=True)
    for i, row in enumerate((1, ROWS - 2)):
        clear, tones = matter(s_ref[row : row + 1], *color)
        for c, v in enumerate((*tones, clear)):
            ends_ref[c, i] = v[0]


def render_outer(splat_ref, x_ref, depth_first_ref, depth_second_ref, zi_ref,
                 ui_ref, wi_ref, api_ref, ami_ref, yi_ref, mid_ref, sides_ref, ends_ref,
                 part_ref, zk_ref, facing_ref, known_ref, z_ref, ap_ref, am_ref, y_ref, s_ref):
    light, color = coefficients(splat_ref)
    odd_group = parity("depth")
    edge_before, edge_after = ends_inside("depth")

    def first(i, _):
        for row in (2 * i, 2 * i + 1):
            ends = [
                by_parity(odd_group, depth_first_ref[k, row], depth_second_ref[k, row])
                for k in range(2)
            ]
            z = binomial([ends[0][0], ends[1][0], cells(x_ref, row, 0), cells(x_ref, row, 1)])
            z += binomial([cells(x_ref, row, 6), cells(x_ref, row, 7), ends[0][1], ends[1][1]])
            z_ref[row, 0] = z[0] * edge_before
            z_ref[row, 1] = z[1]
            z_ref[row, 2] = z[2]
            z_ref[row, 3] = z[3] * edge_after
        return 0

    lax.fori_loop(0, ROWS // 2, first, 0, unroll=True)

    def second(i, _):
        row = PAIR * i + 1
        here = pl.ds(row, PAIR)
        s = smoothed(row_sums(z_ref[pl.ds(row - 1, PAIR + 2)]), 1.0 / 64.0)
        u, w = column_parts(s)
        for side in range(2):
            at = pl.ds(2 * side, 2)
            if side == 0:
                us = jnp.concatenate([u[:, 0:2], ui_ref[here, 0:2]], 1)
                ws = jnp.concatenate([w[:, 0:2], wi_ref[here, 0:2]], 1)
            else:
                us = jnp.concatenate([ui_ref[here, 2:4], u[:, 2:4]], 1)
                ws = jnp.concatenate([wi_ref[here, 2:4], w[:, 2:4]], 1)
            ap_ref[here, at], am_ref[here, at], y_ref[here, at] = gradient_parts(us, ws, light)
        s_ref[here] = s[:, 1:3]
        return 0

    lax.fori_loop(0, (ROWS - 2) // PAIR, second, 0, unroll=True)

    def third(i):
        row = 2 * i + 2
        here = pl.ds(row, 2)
        facing = (ap_ref[pl.ds(row + 1, 2)] + am_ref[pl.ds(row - 1, 2)]) + y_ref[here]
        clear, tones = matter(s_ref[here], *color)
        own, kept = (*tones, clear), [sides_ref[c, here] for c in range(4)]
        front = [jnp.concatenate([a[:, :1], b[:, :1]], 1) for a, b in zip(own, kept)]
        back = [jnp.concatenate([b[:, 1:], a[:, 1:]], 1) for a, b in zip(own, kept)]
        total = shade((front[3], front[:3]), facing[:, 0:2], None)
        total = over(total, [mid_ref[c, here] for c in range(4)])
        total = shade((back[3], back[:3]), facing[:, 2:4], total)
        for c in range(4):
            at = pl.multiple_of((c * ROWS + row) * SUB, SUB)
            part_ref[pl.ds(at, 2 * SUB), :] = turned(total[c], c, i // 3).reshape(2 * SUB, LANE)
        return 0

    for i in range((ROWS - 4) // 2):
        third(i)

    def whole(inner, outer):
        return jnp.concatenate([outer[0:2], inner, outer[2:4]], 0)

    for i, row in enumerate((0, 1, ROWS - 1, ROWS - 2)):
        zk_ref[i] = whole(zi_ref[row], z_ref[row])
    facing_ref[0] = whole(api_ref[1], ap_ref[1])
    facing_ref[1] = whole(api_ref[2] + yi_ref[1], ap_ref[2] + y_ref[1])
    facing_ref[2] = whole(ami_ref[ROWS - 2], am_ref[ROWS - 2])
    facing_ref[3] = whole(ami_ref[ROWS - 3] + yi_ref[ROWS - 2], am_ref[ROWS - 3] + y_ref[ROWS - 2])
    for i, row in enumerate((1, ROWS - 2)):
        clear, tones = matter(s_ref[row : row + 1], *color)
        for c, v in enumerate((*tones, clear)):
            known_ref[c, i, 0] = v[0, 0]
            known_ref[c, i, 1:7] = ends_ref[c, i]
            known_ref[c, i, 7] = v[0, 1]


def render_rows(splat_ref, strip_first_ref, strip_second_ref, _, zk_ref,
                facing_ref, known_ref, out_ref, all_ref, halo_ref):
    light, color = coefficients(splat_ref)
    odd_strip = parity("strip")
    edge_before, edge_after = ends_inside("depth")
    edge_up, edge_down = ends_inside("strip")

    for half, ref in ((1 - odd_strip, strip_first_ref), (odd_strip, strip_second_ref)):
        for j in range(2):
            z = binomial([ref[slab, j] for slab in range(SLABS + 4)])
            z[0] = z[0] * edge_before
            z[-1] = z[-1] * edge_after
            for i, v in enumerate(z):
                halo_ref[3 * half + (1 - 2 * half) * j, i] = v

    for half in range(2):
        sign = 1.0 - 2.0 * half
        inside = (edge_down if half else edge_up) * (1.0 / 64.0)
        outer, inner = halo_ref[2 * half], halo_ref[2 * half + 1]
        first, second = zk_ref[2 * half], zk_ref[2 * half + 1]
        mirrored = [light[0] * sign, light[1], light[2]]

        def row_parts(lower, middle, upper, factor):
            s = smoothed((lower + middle) + (middle + upper), factor)[None]
            return s[:, 1:-1], *gradient_parts(*column_parts(s), mirrored)

        def finish(row, found, facing):
            total = shade(found, facing, None)
            for c in range(4):
                at = (c * ROWS + row) * SUB
                all_ref[at : at + SUB, :] = turned(total[c], c, half)[0]

        _, _, beyond, _ = row_parts(outer, inner, first, inside)
        s, _, inward, own = row_parts(inner, first, second, 1.0 / 64.0)
        finish((ROWS - 1) * half, matter(s, *color), facing_ref[pl.ds(2 * half, 1)] + beyond + own)
        known = [known_ref[c, half : half + 1] for c in range(4)]
        finish(1 + (ROWS - 3) * half, (known[3], known[:3]), facing_ref[pl.ds(2 * half + 1, 1)] + inward)

    chunk = lax.broadcasted_iota(jnp.int32, (SUB, LANE), 1) // 16
    for tile in range(SUB):
        v = [all_ref[pl.ds(g * 64 + tile, SUB, stride=SUB), :] for g in range(8)]
        for bit in (1, 2, 4):
            v = [jnp.where((chunk & bit) != 0, v[(k + bit) % 8], v[k]) for k in range(8)]
        for m in range(8):
            row = (tile * 8 + m) * SUB
            out_ref[row : row + SUB, :] = rolled(v[-m % 8], LANE - 16 * m, 1) if m else v[0]


def composite(parts_ref, out_ref):
    is_clear = lax.broadcasted_iota(jnp.int32, (SUB, LANE), 1) >= 96
    count = parts_ref.shape[0] // SUB
    runs = 4
    through = [jnp.ones((SUB, LANE), jnp.float32)] * runs
    total = [jnp.zeros((SUB, LANE), jnp.float32)] * runs
    for step in range(count // runs):
        for run in range(runs):
            d = run * (count // runs) + step
            x = parts_ref[d * SUB : (d + 1) * SUB, :]
            total[run] = total[run] + through[run] * x
            m = jnp.where(is_clear, x, 1.0)
            m = m * pltpu.roll(m, 32, 1)
            m = m * pltpu.roll(m, 64, 1)
            through[run] = through[run] * m
    image, clear = total[0], through[0]
    for run in range(1, runs):
        image = image + clear * total[run]
        clear = clear * through[run]
    result = jnp.where(is_clear, 1.0 - clear, image)
    for i in range(8):
        moved = result if i == 0 else pltpu.roll(result, LANE - 16 * i, 1)
        out_ref[i * SUB : (i + 1) * SUB, :] = moved[:, 0:16]


def f32(*shape):
    return pltpu.VMEM(shape, jnp.float32)


def near(*arrays):
    return [pltpu.with_memory_space_constraint(a, pltpu.VMEM) for a in arrays]


def local(volume, extinction, color_map, light_direction):
    groups = lax.axis_size("depth")
    x = volume.reshape(ROWS, SLABS, SUB, LANE).transpose(0, 2, 1, 3).reshape(ROWS * 64, LANE)

    def swaps(count):
        out = []
        for start in range(2):
            half = [(i, i + 1) for i in range(start, count - 1, 2)]
            out.append(half + [(b, a) for a, b in half])
        return out

    def exchange(buffers, axis):
        out = []
        for v, p in zip(buffers, swaps(lax.axis_size(axis))):
            out.append(lax.ppermute(v, axis, p))
        return out

    packed = pl.pallas_call(
        pack_depth, in_specs=[pl.BlockSpec(memory_space=pltpu.HBM)], out_specs=[VM, VM],
        compiler_params=SMALL, name="pack_depth",
        out_shape=[f32(2, ROWS * SUB, 1, LANE)] * 2,
        scratch_shapes=[pltpu.SemaphoreType.DMA((2, 2))],
    )(pltpu.with_memory_space_constraint(x.reshape(ROWS * SUB, SLABS, 1, LANE), pltpu.HBM))
    packed = [v.reshape(2, ROWS, SUB, LANE) for v in packed]
    near_depth = exchange(packed, "depth")

    params = (extinction, color_map.T, light_direction)

    def kernel(body, operands, shapes, scratch=(), aliases={}, params=()):
        return pl.pallas_call(
            body, in_specs=[SM] * len(params) + [VM] * len(operands), out_specs=[VM] * len(shapes),
            compiler_params=SMALL, input_output_aliases=aliases, out_shape=[f32(*shape) for shape in shapes],
            scratch_shapes=[f32(*shape) for shape in scratch],
        )(*params, *near(*operands))

    four = (ROWS, 4, SUB, LANE)
    splat, zi, ui, wi, api, ami, yi, _, mid, sides, ends = kernel(
        render_inner, (x, packed[0]),
        [(10, SUB, LANE), (ROWS, 6, SUB, LANE)] + [four] * 5
        + [(ROWS, 6, SUB, LANE), (4, ROWS, SUB, LANE), (4, ROWS, 2, SUB, LANE), (4, 2, 6, SUB, LANE)],
        params=params,
    )
    near_strip = exchange(
        pl.pallas_call(
            pack_strip, in_specs=[VM] * 4, compiler_params=SMALL, out_specs=[VM, VM], name="pack_strip",
            out_shape=[f32(SLABS + 4, 2, SUB, LANE)] * 2,
        )(*near(x, *near_depth, mid)),
        "strip",
    )
    kept = kernel(
        render_outer, (splat, x, *near_depth, zi, ui, wi, api, ami, yi, mid, sides, ends),
        [(4 * ROWS * SUB, LANE), (4, SLABS + 2, SUB, LANE), (4, SLABS, SUB, LANE), (4, 2, SLABS, SUB, LANE)],
        [four] * 4 + [(ROWS, 2, SUB, LANE)],
    )
    blocks, _ = kernel(
        render_rows, (splat, *near_strip, *kept), [(groups * SUB, LANE), (4 * ROWS * SUB, LANE)],
        [(4, SLABS + 2, SUB, LANE)], {3: 1},
    )
    layers = lax.all_to_all(
        blocks.reshape(groups, SUB, LANE), "depth", split_axis=0, concat_axis=0, tiled=True
    )
    image = pl.pallas_call(
        composite, in_specs=[VM], compiler_params=SMALL, out_specs=VM, name="composite",
        out_shape=jax.ShapeDtypeStruct((64, 16), jnp.float32),
    )(*near(layers.reshape(groups * SUB, LANE)))
    return image.reshape(4, 16, 16)


def solution(mesh):
    in_specs = (P("strip", "depth", None), P(), P(), P())
    out_specs = P(None, "strip", "depth")
    return jax.shard_map(local, mesh=mesh, in_specs=in_specs, out_specs=out_specs, check_vma=False)
```

```python
import jax
import jax.numpy as jnp
from jax import lax
from jax.experimental import pallas as pl
from jax.experimental.pallas import tpu as pltpu
from jax.sharding import PartitionSpec as P


ROWS, SLABS, SUB, LANE = 16, 8, 8, 128
PAIR = 2
VM = pl.BlockSpec(memory_space=pltpu.VMEM)


SMALL = pltpu.CompilerParams(vmem_limit_bytes=4 << 20)


def cells(x_ref, row, slab):
    return x_ref[pl.ds(row * 64 + slab, SUB, stride=SLABS), :]


def parity(axis):
    return lax.axis_index(axis) % 2


def pack_depth(x_ref, first_ref, second_ref, sems):
    start = (SLABS - 2) * (1 - parity("depth"))
    copies = []
    for i, (ref, slab) in enumerate(((second_ref, (SLABS - 2) - start), (first_ref, start))):
        for k in range(2):
            copies.append(pltpu.make_async_copy(x_ref.at[:, slab + k], ref.at[k], sems.at[i, k]))
    for copy in copies:
        copy.start()
    for copy in copies:
        copy.wait()


def by_parity(odd, first, second):
    is_odd = odd == 1
    return jnp.where(is_odd, first, second), jnp.where(is_odd, second, first)


def pack_strip(x_ref, from_first_ref, from_second_ref, _, first_ref, second_ref):
    odd = parity("strip")
    group_odd = parity("depth")
    start = (ROWS - 2) * (1 - odd)
    for ref, row in ((first_ref, start), (second_ref, (ROWS - 2) - start)):
        for k in range(2):
            for j in range(2):
                before, after = by_parity(
                    group_odd, from_first_ref[j, row + k], from_second_ref[j, row + k]
                )
                ref[j, k] = before
                ref[SLABS + 2 + j, k] = after
            for slab in range(SLABS):
                ref[2 + slab, k] = cells(x_ref, row + k, slab)


def rolled(v, shift, axis):
    return pltpu.roll(v.reshape(-1, SUB, LANE), shift, axis + 1).reshape(v.shape)


def column_neighbours(v):
    lane = lax.broadcasted_iota(jnp.int32, v.shape, v.ndim - 1)
    sub = lax.broadcasted_iota(jnp.int32, v.shape, v.ndim - 2)
    a = rolled(v, 1, 1)
    prev = jnp.where(lane == 0, jnp.where(sub == 0, 0.0, rolled(a, 1, 0)), a)
    a = rolled(v, LANE - 1, 1)
    following = jnp.where(lane == LANE - 1, jnp.where(sub == SUB - 1, 0.0, rolled(a, SUB - 1, 0)), a)
    return prev, following


def log1p_unit(e):
    w = 1.0 + e
    return jnp.log(w) + (e - (w - 1.0))


def row_sums(z):
    e = z[:-1] + z[1:]
    return e[:-1] + e[1:]


def slab_sums(v):
    e = v[:, :-1] + v[:, 1:]
    return e[:, :-1] + e[:, 1:]


def smoothed(m, factor):
    prev, following = column_neighbours(m)
    return ((prev + following) + (m + m)) * factor


def column_parts(s):
    prev, following = column_neighbours(s)
    return (prev + following) + (s + s), following - prev


def gradient_parts(u, w, light):
    scale = 0.5 * 0.25 * 0.25
    y = (light[1] * scale) * (u[:, 2:] - u[:, :-2]) + (light[2] * scale) * slab_sums(w)
    p = (light[0] * scale) * slab_sums(u)
    return y + p, y - p, y + y


def matter(s, ext, slopes, offsets):
    z = s + s
    soft = jnp.maximum(z, 0.0) + log1p_unit(jnp.exp(-jnp.abs(z)))
    return jnp.exp(-ext * soft), [jnp.tanh(a * s + b) + 1.0 for a, b in zip(slopes, offsets)]


def shade(cells_matter, facing, front):
    clear, tones = cells_matter
    weight = (1.0 - clear) * (0.5 - 0.35 / (1.0 + facing * facing))
    total = front
    for k in range(facing.shape[1]):
        if total is None:
            total = [weight[:, k] * t[:, k] for t in tones] + [clear[:, k]]
        else:
            here = weight[:, k] * total[3]
            total = [c + here * t[:, k] for c, t in zip(total, tones)] + [total[3] * clear[:, k]]
    return total


def over(front, back):
    through = front[3]
    return [f + through * c for f, c in zip(front[:3], back[:3])] + [through * back[3]]


def turned(v, channel, half):
    turn = 16 * (2 * channel + half)
    return rolled(v, turn, 1) if turn else v


def coefficients(splat_ref):
    light, slopes, offsets = ([splat_ref[3 * i + c] for c in range(3)] for i in range(3))
    return light, (splat_ref[9], slopes, offsets)


def ends_inside(axis):
    index, count = lax.axis_index(axis), lax.axis_size(axis)
    return jnp.where(index == 0, 0.0, 1.0), jnp.where(index == count - 1, 0.0, 1.0)


def binomial(v):
    e = [a + b for a, b in zip(v, v[1:])]
    return [a + b for a, b in zip(e, e[1:])]


def render_inner(splat_ref, x_ref, _, z_ref, u_ref, w_ref, ap_ref, am_ref, y_ref,
                 s_ref, mid_ref, sides_ref, ends_ref):
    light, color = coefficients(splat_ref)

    def first(i, _):
        for row in (2 * i, 2 * i + 1):
            z = binomial([cells(x_ref, row, slab) for slab in range(SLABS)])
            for i, v in enumerate(z):
                z_ref[row, i] = v
        return 0

    lax.fori_loop(0, ROWS // 2, first, 0, unroll=True)

    def second(i, _):
        row = PAIR * i + 1
        s = smoothed(row_sums(z_ref[pl.ds(row - 1, PAIR + 2)]), 1.0 / 64.0)
        u, w = column_parts(s)
        here = pl.ds(row, PAIR)
        for i, k in enumerate((0, 1, 4, 5)):
            u_ref[here, i] = u[:, k]
            w_ref[here, i] = w[:, k]
        ap_ref[here], am_ref[here], y_ref[here] = gradient_parts(u, w, light)
        s_ref[here] = s
        return 0

    lax.fori_loop(0, (ROWS - 2) // PAIR, second, 0, unroll=True)

    def third(i, _):
        row = 2 * i + 2
        here = pl.ds(row, 2)
        facing = (ap_ref[pl.ds(row + 1, 2)] + am_ref[pl.ds(row - 1, 2)]) + y_ref[here]
        clear, tones = matter(s_ref[here], *color)
        total = shade((clear[:, 1:5], [t[:, 1:5] for t in tones]), facing, None)
        for c in range(4):
            mid_ref[c, here] = total[c]
        for c, v in enumerate((*tones, clear)):
            sides_ref[c, here, 0] = v[:, 0]
            sides_ref[c, here, 1] = v[:, 5]
        return 0

    lax.fori_loop(0, (ROWS - 4) // 2, third, 0, unroll=True)
    for i, row in enumerate((1, ROWS - 2)):
        clear, tones = matter(s_ref[row : row + 1], *color)
        for c, v in enumerate((*tones, clear)):
            ends_ref[c, i] = v[0]


def render_outer(splat_ref, x_ref, depth_first_ref, depth_second_ref, zi_ref,
                 ui_ref, wi_ref, api_ref, ami_ref, yi_ref, mid_ref, sides_ref, ends_ref,
                 part_ref, zk_ref, facing_ref, known_ref, z_ref, ap_ref, am_ref, y_ref, s_ref):
    light, color = coefficients(splat_ref)
    odd_group = parity("depth")
    edge_before, edge_after = ends_inside("depth")

    def first(i, _):
        for row in (2 * i, 2 * i + 1):
            ends = [
                by_parity(odd_group, depth_first_ref[k, row], depth_second_ref[k, row])
                for k in range(2)
            ]
            z = binomial([ends[0][0], ends[1][0], cells(x_ref, row, 0), cells(x_ref, row, 1)])
            z += binomial([cells(x_ref, row, 6), cells(x_ref, row, 7), ends[0][1], ends[1][1]])
            z_ref[row, 0] = z[0] * edge_before
            z_ref[row, 1] = z[1]
            z_ref[row, 2] = z[2]
            z_ref[row, 3] = z[3] * edge_after
        return 0

    lax.fori_loop(0, ROWS // 2, first, 0, unroll=True)

    def second(i, _):
        row = PAIR * i + 1
        here = pl.ds(row, PAIR)
        s = smoothed(row_sums(z_ref[pl.ds(row - 1, PAIR + 2)]), 1.0 / 64.0)
        u, w = column_parts(s)
        for side in range(2):
            at = pl.ds(2 * side, 2)
            if side == 0:
                us = jnp.concatenate([u[:, 0:2], ui_ref[here, 0:2]], 1)
                ws = jnp.concatenate([w[:, 0:2], wi_ref[here, 0:2]], 1)
            else:
                us = jnp.concatenate([ui_ref[here, 2:4], u[:, 2:4]], 1)
                ws = jnp.concatenate([wi_ref[here, 2:4], w[:, 2:4]], 1)
            ap_ref[here, at], am_ref[here, at], y_ref[here, at] = gradient_parts(us, ws, light)
        s_ref[here] = s[:, 1:3]
        return 0

    lax.fori_loop(0, (ROWS - 2) // PAIR, second, 0, unroll=True)

    def third(i):
        row = 2 * i + 2
        here = pl.ds(row, 2)
        facing = (ap_ref[pl.ds(row + 1, 2)] + am_ref[pl.ds(row - 1, 2)]) + y_ref[here]
        clear, tones = matter(s_ref[here], *color)
        own, kept = (*tones, clear), [sides_ref[c, here] for c in range(4)]
        front = [jnp.concatenate([a[:, :1], b[:, :1]], 1) for a, b in zip(own, kept)]
        back = [jnp.concatenate([b[:, 1:], a[:, 1:]], 1) for a, b in zip(own, kept)]
        total = shade((front[3], front[:3]), facing[:, 0:2], None)
        total = over(total, [mid_ref[c, here] for c in range(4)])
        total = shade((back[3], back[:3]), facing[:, 2:4], total)
        for c in range(4):
            at = pl.multiple_of((c * ROWS + row) * SUB, SUB)
            part_ref[pl.ds(at, 2 * SUB), :] = turned(total[c], c, i // 3).reshape(2 * SUB, LANE)
        return 0

    for i in range((ROWS - 4) // 2):
        third(i)

    def whole(inner, outer):
        return jnp.concatenate([outer[0:2], inner, outer[2:4]], 0)

    for i, row in enumerate((0, 1, ROWS - 1, ROWS - 2)):
        zk_ref[i] = whole(zi_ref[row], z_ref[row])
    facing_ref[0] = whole(api_ref[1], ap_ref[1])
    facing_ref[1] = whole(api_ref[2] + yi_ref[1], ap_ref[2] + y_ref[1])
    facing_ref[2] = whole(ami_ref[ROWS - 2], am_ref[ROWS - 2])
    facing_ref[3] = whole(ami_ref[ROWS - 3] + yi_ref[ROWS - 2], am_ref[ROWS - 3] + y_ref[ROWS - 2])
    for i, row in enumerate((1, ROWS - 2)):
        clear, tones = matter(s_ref[row : row + 1], *color)
        for c, v in enumerate((*tones, clear)):
            known_ref[c, i, 0] = v[0, 0]
            known_ref[c, i, 1:7] = ends_ref[c, i]
            known_ref[c, i, 7] = v[0, 1]


def render_rows(splat_ref, strip_first_ref, strip_second_ref, _, zk_ref,
                facing_ref, known_ref, out_ref, all_ref, halo_ref):
    light, color = coefficients(splat_ref)
    odd_strip = parity("strip")
    edge_before, edge_after = ends_inside("depth")
    edge_up, edge_down = ends_inside("strip")

    for half, ref in ((1 - odd_strip, strip_first_ref), (odd_strip, strip_second_ref)):
        for j in range(2):
            z = binomial([ref[slab, j] for slab in range(SLABS + 4)])
            z[0] = z[0] * edge_before
            z[-1] = z[-1] * edge_after
            for i, v in enumerate(z):
                halo_ref[3 * half + (1 - 2 * half) * j, i] = v

    for half in range(2):
        sign = 1.0 - 2.0 * half
        inside = (edge_down if half else edge_up) * (1.0 / 64.0)
        outer, inner = halo_ref[2 * half], halo_ref[2 * half + 1]
        first, second = zk_ref[2 * half], zk_ref[2 * half + 1]
        mirrored = [light[0] * sign, light[1], light[2]]

        def row_parts(lower, middle, upper, factor):
            s = smoothed((lower + middle) + (middle + upper), factor)[None]
            return s[:, 1:-1], *gradient_parts(*column_parts(s), mirrored)

        def finish(row, found, facing):
            total = shade(found, facing, None)
            for c in range(4):
                at = (c * ROWS + row) * SUB
                all_ref[at : at + SUB, :] = turned(total[c], c, half)[0]

        _, _, beyond, _ = row_parts(outer, inner, first, inside)
        s, _, inward, own = row_parts(inner, first, second, 1.0 / 64.0)
        finish((ROWS - 1) * half, matter(s, *color), facing_ref[pl.ds(2 * half, 1)] + beyond + own)
        known = [known_ref[c, half : half + 1] for c in range(4)]
        finish(1 + (ROWS - 3) * half, (known[3], known[:3]), facing_ref[pl.ds(2 * half + 1, 1)] + inward)

    chunk = lax.broadcasted_iota(jnp.int32, (SUB, LANE), 1) // 16
    for tile in range(SUB):
        v = [all_ref[pl.ds(g * 64 + tile, SUB, stride=SUB), :] for g in range(8)]
        for bit in (1, 2, 4):
            v = [jnp.where((chunk & bit) != 0, v[(k + bit) % 8], v[k]) for k in range(8)]
        for m in range(8):
            row = (tile * 8 + m) * SUB
            out_ref[row : row + SUB, :] = rolled(v[-m % 8], LANE - 16 * m, 1) if m else v[0]


def composite(parts_ref, out_ref):
    is_clear = lax.broadcasted_iota(jnp.int32, (SUB, LANE), 1) >= 96
    count = parts_ref.shape[0] // SUB
    runs = 4
    through = [jnp.ones((SUB, LANE), jnp.float32)] * runs
    total = [jnp.zeros((SUB, LANE), jnp.float32)] * runs
    for step in range(count // runs):
        for run in range(runs):
            d = run * (count // runs) + step
            x = parts_ref[d * SUB : (d + 1) * SUB, :]
            total[run] = total[run] + through[run] * x
            m = jnp.where(is_clear, x, 1.0)
            m = m * pltpu.roll(m, 32, 1)
            m = m * pltpu.roll(m, 64, 1)
            through[run] = through[run] * m
    image, clear = total[0], through[0]
    for run in range(1, runs):
        image = image + clear * total[run]
        clear = clear * through[run]
    result = jnp.where(is_clear, 1.0 - clear, image)
    for i in range(8):
        moved = result if i == 0 else pltpu.roll(result, LANE - 16 * i, 1)
        out_ref[i * SUB : (i + 1) * SUB, :] = moved[:, 0:16]


def f32(*shape):
    return pltpu.VMEM(shape, jnp.float32)


def near(*arrays):
    return [pltpu.with_memory_space_constraint(a, pltpu.VMEM) for a in arrays]


def local(volume, extinction, color_map, light_direction):
    groups = lax.axis_size("depth")
    x = volume.reshape(ROWS, SLABS, SUB, LANE).transpose(0, 2, 1, 3).reshape(ROWS * 64, LANE)

    def swaps(count):
        out = []
        for start in range(2):
            half = [(i, i + 1) for i in range(start, count - 1, 2)]
            out.append(half + [(b, a) for a, b in half])
        return out

    def exchange(buffers, axis):
        out = []
        for v, p in zip(buffers, swaps(lax.axis_size(axis))):
            out.append(lax.ppermute(v, axis, p))
        return out

    packed = pl.pallas_call(
        pack_depth, in_specs=[pl.BlockSpec(memory_space=pltpu.HBM)], out_specs=[VM, VM],
        compiler_params=SMALL, name="pack_depth",
        out_shape=[f32(2, ROWS * SUB, 1, LANE)] * 2,
        scratch_shapes=[pltpu.SemaphoreType.DMA((2, 2))],
    )(pltpu.with_memory_space_constraint(x.reshape(ROWS * SUB, SLABS, 1, LANE), pltpu.HBM))
    packed = [v.reshape(2, ROWS, SUB, LANE) for v in packed]
    near_depth = exchange(packed, "depth")

    values = jnp.concatenate([light_direction, 0.5 * color_map.T.reshape(6), extinction])
    splat = jnp.broadcast_to(values[:, None, None], (10, SUB, LANE))

    def kernel(body, operands, shapes, scratch=(), aliases={}):
        return pl.pallas_call(
            body, in_specs=[VM] * len(operands), out_specs=[VM] * len(shapes),
            compiler_params=SMALL, input_output_aliases=aliases, out_shape=[f32(*shape) for shape in shapes],
            scratch_shapes=[f32(*shape) for shape in scratch],
        )(*near(*operands))

    four = (ROWS, 4, SUB, LANE)
    zi, ui, wi, api, ami, yi, _, mid, sides, ends = kernel(
        render_inner, (splat, x, packed[0]),
        [(ROWS, 6, SUB, LANE)] + [four] * 5
        + [(ROWS, 6, SUB, LANE), (4, ROWS, SUB, LANE), (4, ROWS, 2, SUB, LANE), (4, 2, 6, SUB, LANE)],
    )
    near_strip = exchange(
        pl.pallas_call(
            pack_strip, in_specs=[VM] * 4, compiler_params=SMALL, out_specs=[VM, VM], name="pack_strip",
            out_shape=[f32(SLABS + 4, 2, SUB, LANE)] * 2,
        )(*near(x, *near_depth, mid)),
        "strip",
    )
    kept = kernel(
        render_outer, (splat, x, *near_depth, zi, ui, wi, api, ami, yi, mid, sides, ends),
        [(4 * ROWS * SUB, LANE), (4, SLABS + 2, SUB, LANE), (4, SLABS, SUB, LANE), (4, 2, SLABS, SUB, LANE)],
        [four] * 4 + [(ROWS, 2, SUB, LANE)],
    )
    blocks, _ = kernel(
        render_rows, (splat, *near_strip, *kept), [(groups * SUB, LANE), (4 * ROWS * SUB, LANE)],
        [(4, SLABS + 2, SUB, LANE)], {3: 1},
    )
    layers = lax.all_to_all(
        blocks.reshape(groups, SUB, LANE), "depth", split_axis=0, concat_axis=0, tiled=True
    )
    image = pl.pallas_call(
        composite, in_specs=[VM], compiler_params=SMALL, out_specs=VM, name="composite",
        out_shape=jax.ShapeDtypeStruct((64, 16), jnp.float32),
    )(*near(layers.reshape(groups * SUB, LANE)))
    return image.reshape(4, 16, 16)


def solution(mesh):
    in_specs = (P("strip", "depth", None), P(), P(), P())
    out_specs = P(None, "strip", "depth")
    return jax.shard_map(local, mesh=mesh, in_specs=in_specs, out_specs=out_specs, check_vma=False)
```

```python
import jax
import jax.numpy as jnp
from jax import lax
from jax.experimental import pallas as pl
from jax.experimental.pallas import tpu as pltpu
from jax.sharding import PartitionSpec as P


ROWS, SLABS, SUB, LANE = 16, 8, 8, 128
PAIR = 2
VM = pl.BlockSpec(memory_space=pltpu.VMEM)


SMALL = pltpu.CompilerParams(vmem_limit_bytes=4 << 20)


def cells(x_ref, row, slab):
    return x_ref[pl.ds(row * 64 + slab, SUB, stride=SLABS), :]


def halo_cells(halo_ref, row, k):
    return halo_ref[pl.ds(row * 16 + k, SUB, stride=2), :]


def parity(axis):
    return lax.axis_index(axis) % 2


def pack_depth(x_ref, first_ref, second_ref, sems):
    start = (SLABS - 2) * (1 - parity("depth"))
    copies = []
    for i, (ref, slab) in enumerate(((second_ref, (SLABS - 2) - start), (first_ref, start))):
        copies.append(pltpu.make_async_copy(x_ref.at[:, pl.ds(slab, 2)], ref, sems.at[i]))
    for copy in copies:
        copy.start()
    for copy in copies:
        copy.wait()


def by_parity(odd, first, second):
    is_odd = odd == 1
    return jnp.where(is_odd, first, second), jnp.where(is_odd, second, first)


def pack_strip(x_ref, from_first_ref, from_second_ref, _, first_ref, second_ref):
    odd = parity("strip")
    group_odd = parity("depth")
    start = (ROWS - 2) * (1 - odd)
    for ref, row in ((first_ref, start), (second_ref, (ROWS - 2) - start)):
        for k in range(2):
            for j in range(2):
                before, after = by_parity(
                    group_odd, halo_cells(from_first_ref, row + k, j), halo_cells(from_second_ref, row + k, j)
                )
                ref[j, k] = before
                ref[SLABS + 2 + j, k] = after
            for slab in range(SLABS):
                ref[2 + slab, k] = cells(x_ref, row + k, slab)


def rolled(v, shift, axis):
    return pltpu.roll(v.reshape(-1, SUB, LANE), shift, axis + 1).reshape(v.shape)


def column_neighbours(v):
    lane = lax.broadcasted_iota(jnp.int32, v.shape, v.ndim - 1)
    sub = lax.broadcasted_iota(jnp.int32, v.shape, v.ndim - 2)
    a = rolled(v, 1, 1)
    prev = jnp.where(lane == 0, jnp.where(sub == 0, 0.0, rolled(a, 1, 0)), a)
    a = rolled(v, LANE - 1, 1)
    following = jnp.where(lane == LANE - 1, jnp.where(sub == SUB - 1, 0.0, rolled(a, SUB - 1, 0)), a)
    return prev, following


def log1p_unit(e):
    w = 1.0 + e
    return jnp.log(w) + (e - (w - 1.0))


def row_sums(z):
    e = z[:-1] + z[1:]
    return e[:-1] + e[1:]


def slab_sums(v):
    e = v[:, :-1] + v[:, 1:]
    return e[:, :-1] + e[:, 1:]


def smoothed(m, factor):
    prev, following = column_neighbours(m)
    return ((prev + following) + (m + m)) * factor


def column_parts(s):
    prev, following = column_neighbours(s)
    return (prev + following) + (s + s), following - prev


def gradient_parts(u, w, light):
    scale = 0.5 * 0.25 * 0.25
    y = (light[1] * scale) * (u[:, 2:] - u[:, :-2]) + (light[2] * scale) * slab_sums(w)
    p = (light[0] * scale) * slab_sums(u)
    return y + p, y - p, y + y


def matter(s, ext, slopes, offsets):
    z = s + s
    soft = jnp.maximum(z, 0.0) + log1p_unit(jnp.exp(-jnp.abs(z)))
    return jnp.exp(-ext * soft), [jnp.tanh(a * s + b) + 1.0 for a, b in zip(slopes, offsets)]


def shade(cells_matter, facing, front):
    clear, tones = cells_matter
    weight = (1.0 - clear) * (0.5 - 0.35 / (1.0 + facing * facing))
    total = front
    for k in range(facing.shape[1]):
        if total is None:
            total = [weight[:, k] * t[:, k] for t in tones] + [clear[:, k]]
        else:
            here = weight[:, k] * total[3]
            total = [c + here * t[:, k] for c, t in zip(total, tones)] + [total[3] * clear[:, k]]
    return total


def over(front, back):
    through = front[3]
    return [f + through * c for f, c in zip(front[:3], back[:3])] + [through * back[3]]


def turned(v, channel, half):
    turn = 16 * (2 * channel + half)
    return rolled(v, turn, 1) if turn else v


def coefficients(splat_ref):
    light, slopes, offsets = ([splat_ref[3 * i + c] for c in range(3)] for i in range(3))
    return light, (splat_ref[9], slopes, offsets)


def ends_inside(axis):
    index, count = lax.axis_index(axis), lax.axis_size(axis)
    return jnp.where(index == 0, 0.0, 1.0), jnp.where(index == count - 1, 0.0, 1.0)


def binomial(v):
    e = [a + b for a, b in zip(v, v[1:])]
    return [a + b for a, b in zip(e, e[1:])]


def render_inner(splat_ref, x_ref, _, z_ref, u_ref, w_ref, ap_ref, am_ref, y_ref,
                 s_ref, mid_ref, sides_ref, ends_ref):
    light, color = coefficients(splat_ref)

    def first(i, _):
        for row in (2 * i, 2 * i + 1):
            z = binomial([cells(x_ref, row, slab) for slab in range(SLABS)])
            for i, v in enumerate(z):
                z_ref[row, i] = v
        return 0

    lax.fori_loop(0, ROWS // 2, first, 0, unroll=True)

    def second(i, _):
        row = PAIR * i + 1
        s = smoothed(row_sums(z_ref[pl.ds(row - 1, PAIR + 2)]), 1.0 / 64.0)
        u, w = column_parts(s)
        here = pl.ds(row, PAIR)
        for i, k in enumerate((0, 1, 4, 5)):
            u_ref[here, i] = u[:, k]
            w_ref[here, i] = w[:, k]
        ap_ref[here], am_ref[here], y_ref[here] = gradient_parts(u, w, light)
        s_ref[here] = s
        return 0

    lax.fori_loop(0, (ROWS - 2) // PAIR, second, 0, unroll=True)

    def third(i, _):
        row = 2 * i + 2
        here = pl.ds(row, 2)
        facing = (ap_ref[pl.ds(row + 1, 2)] + am_ref[pl.ds(row - 1, 2)]) + y_ref[here]
        clear, tones = matter(s_ref[here], *color)
        total = shade((clear[:, 1:5], [t[:, 1:5] for t in tones]), facing, None)
        for c in range(4):
            mid_ref[c, here] = total[c]
        for c, v in enumerate((*tones, clear)):
            sides_ref[c, here, 0] = v[:, 0]
            sides_ref[c, here, 1] = v[:, 5]
        return 0

    lax.fori_loop(0, (ROWS - 4) // 2, third, 0, unroll=True)
    for i, row in enumerate((1, ROWS - 2)):
        clear, tones = matter(s_ref[row : row + 1], *color)
        for c, v in enumerate((*tones, clear)):
            ends_ref[c, i] = v[0]


def render_outer(splat_ref, x_ref, depth_first_ref, depth_second_ref, zi_ref,
                 ui_ref, wi_ref, api_ref, ami_ref, yi_ref, mid_ref, sides_ref, ends_ref,
                 part_ref, zk_ref, facing_ref, known_ref, z_ref, ap_ref, am_ref, y_ref, s_ref):
    light, color = coefficients(splat_ref)
    odd_group = parity("depth")
    edge_before, edge_after = ends_inside("depth")

    def first(i, _):
        for row in (2 * i, 2 * i + 1):
            ends = [
                by_parity(odd_group, halo_cells(depth_first_ref, row, k), halo_cells(depth_second_ref, row, k))
                for k in range(2)
            ]
            z = binomial([ends[0][0], ends[1][0], cells(x_ref, row, 0), cells(x_ref, row, 1)])
            z += binomial([cells(x_ref, row, 6), cells(x_ref, row, 7), ends[0][1], ends[1][1]])
            z_ref[row, 0] = z[0] * edge_before
            z_ref[row, 1] = z[1]
            z_ref[row, 2] = z[2]
            z_ref[row, 3] = z[3] * edge_after
        return 0

    lax.fori_loop(0, ROWS // 2, first, 0, unroll=True)

    def second(i, _):
        row = PAIR * i + 1
        here = pl.ds(row, PAIR)
        s = smoothed(row_sums(z_ref[pl.ds(row - 1, PAIR + 2)]), 1.0 / 64.0)
        u, w = column_parts(s)
        for side in range(2):
            at = pl.ds(2 * side, 2)
            if side == 0:
                us = jnp.concatenate([u[:, 0:2], ui_ref[here, 0:2]], 1)
                ws = jnp.concatenate([w[:, 0:2], wi_ref[here, 0:2]], 1)
            else:
                us = jnp.concatenate([ui_ref[here, 2:4], u[:, 2:4]], 1)
                ws = jnp.concatenate([wi_ref[here, 2:4], w[:, 2:4]], 1)
            ap_ref[here, at], am_ref[here, at], y_ref[here, at] = gradient_parts(us, ws, light)
        s_ref[here] = s[:, 1:3]
        return 0

    lax.fori_loop(0, (ROWS - 2) // PAIR, second, 0, unroll=True)

    def third(i):
        row = 2 * i + 2
        here = pl.ds(row, 2)
        facing = (ap_ref[pl.ds(row + 1, 2)] + am_ref[pl.ds(row - 1, 2)]) + y_ref[here]
        clear, tones = matter(s_ref[here], *color)
        own, kept = (*tones, clear), [sides_ref[c, here] for c in range(4)]
        front = [jnp.concatenate([a[:, :1], b[:, :1]], 1) for a, b in zip(own, kept)]
        back = [jnp.concatenate([b[:, 1:], a[:, 1:]], 1) for a, b in zip(own, kept)]
        total = shade((front[3], front[:3]), facing[:, 0:2], None)
        total = over(total, [mid_ref[c, here] for c in range(4)])
        total = shade((back[3], back[:3]), facing[:, 2:4], total)
        for c in range(4):
            at = pl.multiple_of((c * ROWS + row) * SUB, SUB)
            part_ref[pl.ds(at, 2 * SUB), :] = turned(total[c], c, i // 3).reshape(2 * SUB, LANE)
        return 0

    for i in range((ROWS - 4) // 2):
        third(i)

    def whole(inner, outer):
        return jnp.concatenate([outer[0:2], inner, outer[2:4]], 0)

    for i, row in enumerate((0, 1, ROWS - 1, ROWS - 2)):
        zk_ref[i] = whole(zi_ref[row], z_ref[row])
    facing_ref[0] = whole(api_ref[1], ap_ref[1])
    facing_ref[1] = whole(api_ref[2] + yi_ref[1], ap_ref[2] + y_ref[1])
    facing_ref[2] = whole(ami_ref[ROWS - 2], am_ref[ROWS - 2])
    facing_ref[3] = whole(ami_ref[ROWS - 3] + yi_ref[ROWS - 2], am_ref[ROWS - 3] + y_ref[ROWS - 2])
    for i, row in enumerate((1, ROWS - 2)):
        clear, tones = matter(s_ref[row : row + 1], *color)
        for c, v in enumerate((*tones, clear)):
            known_ref[c, i, 0] = v[0, 0]
            known_ref[c, i, 1:7] = ends_ref[c, i]
            known_ref[c, i, 7] = v[0, 1]


def render_rows(splat_ref, strip_first_ref, strip_second_ref, _, zk_ref,
                facing_ref, known_ref, out_ref, all_ref, halo_ref):
    light, color = coefficients(splat_ref)
    odd_strip = parity("strip")
    edge_before, edge_after = ends_inside("depth")
    edge_up, edge_down = ends_inside("strip")

    for half, ref in ((1 - odd_strip, strip_first_ref), (odd_strip, strip_second_ref)):
        for j in range(2):
            z = binomial([ref[slab, j] for slab in range(SLABS + 4)])
            z[0] = z[0] * edge_before
            z[-1] = z[-1] * edge_after
            for i, v in enumerate(z):
                halo_ref[3 * half + (1 - 2 * half) * j, i] = v

    for half in range(2):
        sign = 1.0 - 2.0 * half
        inside = (edge_down if half else edge_up) * (1.0 / 64.0)
        outer, inner = halo_ref[2 * half], halo_ref[2 * half + 1]
        first, second = zk_ref[2 * half], zk_ref[2 * half + 1]
        mirrored = [light[0] * sign, light[1], light[2]]

        def row_parts(lower, middle, upper, factor):
            s = smoothed((lower + middle) + (middle + upper), factor)[None]
            return s[:, 1:-1], *gradient_parts(*column_parts(s), mirrored)

        def finish(row, found, facing):
            total = shade(found, facing, None)
            for c in range(4):
                at = (c * ROWS + row) * SUB
                all_ref[at : at + SUB, :] = turned(total[c], c, half)[0]

        _, _, beyond, _ = row_parts(outer, inner, first, inside)
        s, _, inward, own = row_parts(inner, first, second, 1.0 / 64.0)
        finish((ROWS - 1) * half, matter(s, *color), facing_ref[pl.ds(2 * half, 1)] + beyond + own)
        known = [known_ref[c, half : half + 1] for c in range(4)]
        finish(1 + (ROWS - 3) * half, (known[3], known[:3]), facing_ref[pl.ds(2 * half + 1, 1)] + inward)

    chunk = lax.broadcasted_iota(jnp.int32, (SUB, LANE), 1) // 16
    for tile in range(SUB):
        v = [all_ref[pl.ds(g * 64 + tile, SUB, stride=SUB), :] for g in range(8)]
        for bit in (1, 2, 4):
            v = [jnp.where((chunk & bit) != 0, v[(k + bit) % 8], v[k]) for k in range(8)]
        for m in range(8):
            row = (tile * 8 + m) * SUB
            out_ref[row : row + SUB, :] = rolled(v[-m % 8], LANE - 16 * m, 1) if m else v[0]


def composite(parts_ref, out_ref):
    is_clear = lax.broadcasted_iota(jnp.int32, (SUB, LANE), 1) >= 96
    count = parts_ref.shape[0] // SUB
    runs = 4
    through = [jnp.ones((SUB, LANE), jnp.float32)] * runs
    total = [jnp.zeros((SUB, LANE), jnp.float32)] * runs
    for step in range(count // runs):
        for run in range(runs):
            d = run * (count // runs) + step
            x = parts_ref[d * SUB : (d + 1) * SUB, :]
            total[run] = total[run] + through[run] * x
            m = jnp.where(is_clear, x, 1.0)
            m = m * pltpu.roll(m, 32, 1)
            m = m * pltpu.roll(m, 64, 1)
            through[run] = through[run] * m
    image, clear = total[0], through[0]
    for run in range(1, runs):
        image = image + clear * total[run]
        clear = clear * through[run]
    result = jnp.where(is_clear, 1.0 - clear, image)
    for i in range(8):
        moved = result if i == 0 else pltpu.roll(result, LANE - 16 * i, 1)
        out_ref[i * SUB : (i + 1) * SUB, :] = moved[:, 0:16]


def f32(*shape):
    return pltpu.VMEM(shape, jnp.float32)


def near(*arrays):
    return [pltpu.with_memory_space_constraint(a, pltpu.VMEM) for a in arrays]


def local(volume, extinction, color_map, light_direction):
    groups = lax.axis_size("depth")
    x = volume.reshape(ROWS, SLABS, SUB, LANE).transpose(0, 2, 1, 3).reshape(ROWS * 64, LANE)

    def swaps(count):
        out = []
        for start in range(2):
            half = [(i, i + 1) for i in range(start, count - 1, 2)]
            out.append(half + [(b, a) for a, b in half])
        return out

    def exchange(buffers, axis):
        out = []
        for v, p in zip(buffers, swaps(lax.axis_size(axis))):
            out.append(lax.ppermute(v, axis, p))
        return out

    packed = pl.pallas_call(
        pack_depth, in_specs=[pl.BlockSpec(memory_space=pltpu.HBM)], out_specs=[VM, VM],
        compiler_params=SMALL, name="pack_depth",
        out_shape=[f32(ROWS * SUB, 2, 1, LANE)] * 2,
        scratch_shapes=[pltpu.SemaphoreType.DMA((2,))],
    )(pltpu.with_memory_space_constraint(x.reshape(ROWS * SUB, SLABS, 1, LANE), pltpu.HBM))
    packed = [v.reshape(2 * ROWS * SUB, LANE) for v in packed]
    near_depth = exchange(packed, "depth")

    values = jnp.concatenate([light_direction, 0.5 * color_map.T.reshape(6), extinction])
    splat = jnp.broadcast_to(values[:, None, None], (10, SUB, LANE))

    def kernel(body, operands, shapes, scratch=(), aliases={}):
        return pl.pallas_call(
            body, in_specs=[VM] * len(operands), out_specs=[VM] * len(shapes),
            compiler_params=SMALL, input_output_aliases=aliases, out_shape=[f32(*shape) for shape in shapes],
            scratch_shapes=[f32(*shape) for shape in scratch],
        )(*near(*operands))

    four = (ROWS, 4, SUB, LANE)
    zi, ui, wi, api, ami, yi, _, mid, sides, ends = kernel(
        render_inner, (splat, x, packed[0]),
        [(ROWS, 6, SUB, LANE)] + [four] * 5
        + [(ROWS, 6, SUB, LANE), (4, ROWS, SUB, LANE), (4, ROWS, 2, SUB, LANE), (4, 2, 6, SUB, LANE)],
    )
    near_strip = exchange(
        pl.pallas_call(
            pack_strip, in_specs=[VM] * 4, compiler_params=SMALL, out_specs=[VM, VM], name="pack_strip",
            out_shape=[f32(SLABS + 4, 2, SUB, LANE)] * 2,
        )(*near(x, *near_depth, mid)),
        "strip",
    )
    kept = kernel(
        render_outer, (splat, x, *near_depth, zi, ui, wi, api, ami, yi, mid, sides, ends),
        [(4 * ROWS * SUB, LANE), (4, SLABS + 2, SUB, LANE), (4, SLABS, SUB, LANE), (4, 2, SLABS, SUB, LANE)],
        [four] * 4 + [(ROWS, 2, SUB, LANE)],
    )
    blocks, _ = kernel(
        render_rows, (splat, *near_strip, *kept), [(groups * SUB, LANE), (4 * ROWS * SUB, LANE)],
        [(4, SLABS + 2, SUB, LANE)], {3: 1},
    )
    layers = lax.all_to_all(
        blocks.reshape(groups, SUB, LANE), "depth", split_axis=0, concat_axis=0, tiled=True
    )
    image = pl.pallas_call(
        composite, in_specs=[VM], compiler_params=SMALL, out_specs=VM, name="composite",
        out_shape=jax.ShapeDtypeStruct((64, 16), jnp.float32),
    )(*near(layers.reshape(groups * SUB, LANE)))
    return image.reshape(4, 16, 16)


def solution(mesh):
    in_specs = (P("strip", "depth", None), P(), P(), P())
    out_specs = P(None, "strip", "depth")
    return jax.shard_map(local, mesh=mesh, in_specs=in_specs, out_specs=out_specs, check_vma=False)
```
